32 devices in a mesh: dp: 4 (over y, x), tensor: 8 (over z, core).
Axes of the slice: x: 2, y: 2, z: 4, core: 2. Of those that a mesh axis runs over, the one named last changes fastest.
Arguments:
- tokens: bfloat16 [512, 8192], P('dp', 'tensor'), may hold values from -6 to 6
- cotangent: bfloat16 [512, 8192], P('dp', 'tensor'), may hold values from -6 to 6
- up_blocks: bfloat16 [64, 6, 256, 256], P('tensor'), may hold values from -0.15625 to 0.15625
- down_blocks: bfloat16 [64, 6, 256, 256], P('tensor'), may hold values from -0.109375 to 0.109375
- up_left: bfloat16 [8192, 256], P('tensor'), may hold values from -0.0625 to 0.0625
- up_right: bfloat16 [256, 16384], P(None, 'tensor'), may hold values from -0.375 to 0.375
- down_left: bfloat16 [16384, 256], P('tensor'), may hold values from -0.046875 to 0.046875
- down_right: bfloat16 [256, 8192], P(None, 'tensor'), may hold values from -0.375 to 0.375
Outputs:
- layer_out: bfloat16 [512, 8192], P('dp', 'tensor')
- token_grads: bfloat16 [512, 8192], P('dp', 'tensor')
- grad_up_blocks: bfloat16 [64, 6, 256, 256], P('tensor', None, 'dp')
- grad_down_blocks: bfloat16 [64, 6, 256, 256], P('tensor', None, 'dp')
- grad_up_left: bfloat16 [8192, 256], P('tensor', 'dp')
- grad_up_right: bfloat16 [256, 16384], P('dp', 'tensor')
- grad_down_left: bfloat16 [16384, 256], P('tensor', 'dp')
- grad_down_right: bfloat16 [256, 8192], P('dp', 'tensor')
The draws below stay inside these ranges and needn't reach their ends.
All inputs are finite; a program needn't handle non-finite values.
Results may differ from the reference program's by a relative error of at most 0.018.
Values may be sent and summed in bfloat16 or wider, within the bound.
No kernel may reach another device: no remote copies, remote signals or barrier semaphores. Data moves between devices by JAX's collectives and lax.ppermute only.
A program may use at most 128 MiB of HBM per device.

```python
import math
import jax
import jax.numpy as jnp
from jax import lax

D = 8192
FF = 16384
BLK = 256
RANK = 256
FACTORS = 6
TOK_DEV = 128
TOKENS = 512
NM = 32
NH = 64
RATIO = 2


def block_levels(own_key, extent, cuts, low, top_value):
    level, own = 1.0, jax.random.fold_in(own_key, 6)
    for position, shards_of in cuts:
        heights = jnp.exp(jax.random.uniform(jax.random.fold_in(own, position), (shards_of,), jnp.float32, low / len(cuts), top_value / len(cuts)))
        level = level * jnp.repeat(heights, extent[position] // shards_of).reshape([-1 if axis == position else 1 for axis in range(len(extent))])
    return level


def noise(rng, dims, width, most, split=(), held_as=jnp.bfloat16):
    drawn = jax.random.normal(rng, dims, jnp.float32) * width
    if len(split) > 0:
        drawn = block_levels(rng, dims, split, -0.22, 0.18) * drawn
    return jnp.clip(drawn, min=-most, max=most).astype(held_as)


def setup_inputs(seed: int = 0) -> dict:
    keys = jax.random.split(jax.random.key(seed), 9)
    tokens = noise(keys[0], (TOKENS, D), 1.0, 6.0, ((0, 4), (1, 8)))
    cotangent = noise(keys[1], (TOKENS, D), 1.0, 6.0, ((0, 4), (1, 8)))
    up_blocks = noise(keys[2], (NH, FACTORS, BLK, BLK), (FACTORS * BLK) ** -0.5, 0.15625, ((0, 8),))
    down_blocks = noise(keys[3], (NH, FACTORS, BLK, BLK), (FACTORS * RATIO * BLK) ** -0.5, 0.109375, ((0, 8),))
    up_left = noise(keys[4], (D, RANK), D ** -0.5, 0.0625, ((0, 8),))
    up_right = noise(keys[5], (RANK, FF), RANK ** -0.5, 0.375, ((1, 8),))
    down_left = noise(keys[6], (FF, RANK), FF ** -0.5, 0.046875, ((0, 8),))
    down_right = noise(keys[7], (RANK, D), RANK ** -0.5, 0.375, ((1, 8),))
    return {"tokens": tokens, "cotangent": cotangent, "up_blocks": up_blocks, "down_blocks": down_blocks, "up_left": up_left, "up_right": up_right, "down_left": down_left, "down_right": down_right}


butterfly_strides = (0, 1, 2, 4, 8, 16)
root_coef = math.sqrt(2.0 / math.pi)
cubic_coef = 0.044715

def gelu_value(value):
    inner = root_coef * (value + cubic_coef * value * value * value)
    return 0.5 * value * (1.0 + jnp.tanh(inner))

def gelu_slope(value):
    tanh_val = jnp.tanh(root_coef * (value + cubic_coef * value * value * value))
    return 0.5 * (1.0 + tanh_val) + 0.5 * value * (1.0 - tanh_val * tanh_val) * root_coef * (1.0 + 3.0 * cubic_coef * value * value)

def partner_stack(blocks):
    model_ids = jnp.arange(NM, dtype=jnp.int32)
    pieces = [jnp.take(blocks, jnp.bitwise_xor(model_ids, jnp.int32(stride)).astype(jnp.int32), axis=1) for stride in butterfly_strides]
    return jnp.stack(pieces, axis=2)

def partner_sum(parts):
    model_ids = jnp.arange(NM, dtype=jnp.int32)
    total = jnp.zeros((parts.shape[0], NM, BLK), jnp.float32)
    for factor, stride in enumerate(butterfly_strides):
        total = total + jnp.take(parts[:, :, factor], jnp.bitwise_xor(model_ids, jnp.int32(stride)).astype(jnp.int32), axis=1)
    return total

def group_pass(tok_rows, cot_rows, up_w, down_w, up_left, up_right, down_left, down_right):
    f32 = jnp.float32
    bf16 = jnp.bfloat16
    rows = tok_rows.shape[0]
    tok_blocks = partner_stack(tok_rows.reshape(rows, NM, BLK)).astype(f32)
    cot_blocks = partner_stack(cot_rows.reshape(rows, NM, BLK)).astype(f32)
    lat_up = jnp.dot(tok_rows, up_left, preferred_element_type=f32).astype(bf16)
    pre_act = jnp.einsum('tijb,irjbc->tirc', tok_blocks, up_w).reshape(rows, FF)
    pre_act = pre_act + jnp.dot(lat_up, up_right, preferred_element_type=f32)
    act_out = gelu_value(pre_act).astype(bf16)
    lat_down = jnp.dot(act_out, down_left, preferred_element_type=f32).astype(bf16)
    act_four = act_out.astype(f32).reshape(rows, NM, RATIO, BLK)
    parts = jnp.einsum('tirc,irjcb->tijb', act_four, down_w)
    layer_out = partner_sum(parts).reshape(rows, D) + jnp.dot(lat_down, down_right, preferred_element_type=f32)
    lat_cot = jnp.dot(cot_rows, down_right.T, preferred_element_type=f32).astype(bf16)
    act_grad = jnp.einsum('tijb,irjcb->tirc', cot_blocks, down_w).reshape(rows, FF)
    act_grad = act_grad + jnp.dot(lat_cot, down_left.T, preferred_element_type=f32)
    pre_grad = (act_grad * gelu_slope(pre_act)).astype(bf16)
    lat_pre = jnp.dot(pre_grad, up_right.T, preferred_element_type=f32).astype(bf16)
    pre_four = pre_grad.astype(f32).reshape(rows, NM, RATIO, BLK)
    back_parts = jnp.einsum('tirc,irjbc->tijb', pre_four, up_w)
    token_grads = partner_sum(back_parts).reshape(rows, D) + jnp.dot(lat_pre, up_left.T, preferred_element_type=f32)
    grad_up = jnp.einsum('tijb,tirc->irjbc', tok_blocks, pre_four).reshape(NH, FACTORS, BLK, BLK)
    grad_down = jnp.einsum('tirc,tijb->irjcb', act_four, cot_blocks).reshape(NH, FACTORS, BLK, BLK)
    grad_ul = jnp.dot(tok_rows.T, lat_pre, preferred_element_type=f32)
    grad_ur = jnp.dot(lat_up.T, pre_grad, preferred_element_type=f32)
    grad_dl = jnp.dot(act_out.T, lat_cot, preferred_element_type=f32)
    grad_dr = jnp.dot(lat_down.T, cot_rows, preferred_element_type=f32)
    outputs = (layer_out.astype(bf16), token_grads.astype(bf16))
    return (outputs, (grad_up, grad_down, grad_ul, grad_ur, grad_dl, grad_dr))

def reference(tokens, cotangent, up_blocks, down_blocks, up_left, up_right, down_left, down_right):
    f32 = jnp.float32
    bf16 = jnp.bfloat16
    up_w = up_blocks.astype(f32).reshape(NM, RATIO, FACTORS, BLK, BLK)
    down_w = down_blocks.astype(f32).reshape(NM, RATIO, FACTORS, BLK, BLK)
    groups = TOKENS // TOK_DEV
    tok_groups = tokens.reshape(groups, TOK_DEV, D)
    cot_groups = cotangent.reshape(groups, TOK_DEV, D)
    scale = 1.0 / math.sqrt(TOKENS)

    def step_fn(totals, pair):
        outputs, grads = group_pass(pair[0], pair[1], up_w, down_w, up_left, up_right, down_left, down_right)
        rounded = tuple((lax.optimization_barrier((grad * scale).astype(bf16)).astype(f32) for grad in grads))
        return (tuple((first + second for first, second in zip(totals, rounded))), outputs)
    init = (jnp.zeros((NH, FACTORS, BLK, BLK), f32), jnp.zeros((NH, FACTORS, BLK, BLK), f32), jnp.zeros((D, RANK), f32), jnp.zeros((RANK, FF), f32), jnp.zeros((FF, RANK), f32), jnp.zeros((RANK, D), f32))
    totals, outputs = lax.scan(step_fn, init, (tok_groups, cot_groups))
    layer_out = outputs[0].reshape(TOKENS, D)
    token_grads = outputs[1].reshape(TOKENS, D)
    return (layer_out, token_grads, totals[0].astype(bf16), totals[1].astype(bf16), totals[2].astype(bf16), totals[3].astype(bf16), totals[4].astype(bf16), totals[5].astype(bf16))
```

```python
import functools
import math

import jax
import jax.numpy as jnp
from jax import lax
from jax.experimental import pallas as pl
from jax.experimental.pallas import tpu as pltpu
from jax.sharding import PartitionSpec as P

STRIDES = (0, 1, 2, 4, 8, 16)
ROOT = math.sqrt(2.0 / math.pi)
CUBIC = 0.044715
F32 = jnp.float32
BF16 = jnp.bfloat16


def swapped(x, axis, mask):
    return lax.ppermute(x, axis, [(i, i ^ mask) for i in range(lax.axis_size(axis))])


def spread(x, order):
    got = {0: x}
    for mask in order:
        for m in list(got):
            got[m ^ mask] = swapped(got[m], "dp", mask)
    return [got[m] for m in range(len(got))]


def total(x):
    mask = lax.axis_size("tensor") // 2
    while mask:
        x = (x.astype(F32) + swapped(x, "tensor", mask).astype(F32)).astype(BF16)
        mask //= 2
    return x


def nn(a, b):
    return jnp.dot(a, b, preferred_element_type=F32)


def nt(a, b):
    return lax.dot_general(a, b, (((1,), (1,)), ((), ())), preferred_element_type=F32)


def main_kernel(near, far, ratio, blk, *refs):
    n = far
    tok, cot = refs[0], refs[1]
    tok_far, cot_far = refs[2 : 2 + n], refs[2 + n : 2 + 2 * n]
    lat, up, down, ur, dl = refs[2 + 2 * n : 7 + 2 * n]
    act, pre, here, *rest = refs[7 + 2 * n :]
    parts, lat_out = rest[:n], rest[n]
    lat_up, lat_cot, acc_down, acc_pre = rest[n + 1 :]
    rows = tok.shape[0]
    a = pl.program_id(0)

    def cols(block):
        return pl.ds(pl.multiple_of(block * blk, blk), blk)

    @pl.when(a == 0)
    def _():
        lat_up[...] = lat[:, :rows].T
        lat_cot[...] = lat[:, rows:].T
        acc_down[...] = jnp.zeros_like(acc_down)
        acc_pre[...] = jnp.zeros_like(acc_pre)
        here[...] = jnp.zeros_like(here)

    at = [cols(jnp.bitwise_xor(a, s)) for s in near]
    own = cols(a)
    x = jnp.concatenate([tok[:, c] for c in at] + [t[:, own] for t in tok_far], axis=1)
    acts, pres = [], []
    for r in range(ratio):
        sl = slice(r * blk, (r + 1) * blk)
        v = nn(lat_up[...], ur[:, sl]) + nn(x, up[r].reshape(-1, blk))
        g = nt(lat_cot[...], dl[sl, :])
        for j, c in enumerate(at):
            g = g + nt(cot[:, c], down[r, j])
        for j, ref in enumerate(cot_far):
            g = g + nt(ref[:, own], down[r, len(at) + j])
        th = jnp.tanh(ROOT * (v + CUBIC * v * v * v))
        y = (0.5 * v * (1.0 + th)).astype(BF16)
        slope = 0.5 * (1.0 + th) + 0.5 * v * (1.0 - th * th) * ROOT * (1.0 + 3.0 * CUBIC * v * v)
        d = (g * slope).astype(BF16)
        act[:, sl] = y
        pre[:, sl] = d
        acc_down[...] += nn(y, dl[sl, :])
        acc_pre[...] += nt(d, ur[:, sl])
        acts.append(y)
        pres.append(d)
    for j in range(len(at) + n):
        f = sum(nn(acts[r], down[r, j]) for r in range(ratio))
        b = sum(nt(pres[r], up[r, j]) for r in range(ratio))
        if j < len(at):
            here[:rows, at[j]] += f
            here[rows:, at[j]] += b
        else:
            parts[j - len(at)][:rows, :] = f.astype(BF16)
            parts[j - len(at)][rows:, :] = b.astype(BF16)

    @pl.when(a == pl.num_programs(0) - 1)
    def _():
        lat_out[:, :rows] = acc_down[...].T.astype(BF16)
        lat_out[:, rows:] = acc_pre[...].T.astype(BF16)


def main_pass(tok, cot, tok_far, cot_far, lat, up, down, ur, dl, near):
    rows, width = tok.shape
    hidden, factors, blk = up.shape[:3]
    blocks = width // blk
    ratio = hidden // blocks
    rank = dl.shape[1]
    n = len(tok_far)

    def whole(shape):
        return pl.BlockSpec(shape, lambda a: (0,) * len(shape))

    wspec = pl.BlockSpec((ratio, factors, blk, blk), lambda a: (a, 0, 0, 0))
    hspec = pl.BlockSpec((rows, ratio * blk), lambda a: (0, a))
    return pl.pallas_call(
        functools.partial(main_kernel, near, n, ratio, blk),
        grid=(blocks,),
        in_specs=[whole((rows, width))] * (2 + 2 * n)
        + [whole((rank, 2 * rows)), wspec, wspec]
        + [pl.BlockSpec((rank, ratio * blk), lambda a: (0, a)), pl.BlockSpec((ratio * blk, rank), lambda a: (a, 0))],
        out_specs=[hspec, hspec, whole((2 * rows, width))]
        + [pl.BlockSpec((2 * rows, blk), lambda a: (0, a))] * n
        + [whole((rank, 2 * rows))],
        out_shape=[jax.ShapeDtypeStruct((rows, hidden * blk), BF16)] * 2
        + [jax.ShapeDtypeStruct((2 * rows, width), F32)]
        + [jax.ShapeDtypeStruct((2 * rows, width), BF16)] * n
        + [jax.ShapeDtypeStruct((rank, 2 * rows), BF16)],
        scratch_shapes=[pltpu.VMEM((rows, rank), BF16)] * 2 + [pltpu.VMEM((rows, rank), F32)] * 2,
        compiler_params=pltpu.CompilerParams(vmem_limit_bytes=48 * 2**20),
        name="main_pass",
    )(tok, cot, *tok_far, *cot_far, lat, up, down, ur, dl)


def gather_copies(groups, scratch, sem):
    made, at = [], 0
    for refs, dst in zip(groups, scratch):
        rows = refs[0].shape[0]
        some = []
        for m, ref in enumerate(refs):
            some.append(pltpu.make_async_copy(ref, dst.at[pl.ds(m * rows, rows), :], sem.at[at]))
            at += 1
        made.append(some)
    for some in made:
        for c in some:
            c.start()
    return made


def down_kernel(near, n, dp, ratio, blk, scale, *refs):
    take = iter(refs)
    acts = [next(take) for _ in range(dp)]
    cots = [[next(take) for _ in range(dp)] for _ in range(1 + n)]
    lats = [next(take) for _ in range(dp)]
    gd, gdl, act_all = next(take), next(take), next(take)
    cot_all = [next(take) for _ in range(1 + n)]
    act_t, sem = next(take), next(take)
    rows = lats[0].shape[1] // 2
    blocks = cots[0][0].shape[1] // blk
    part = gd.shape[2]
    k = lax.axis_index("dp")
    made = gather_copies([acts] + cots, [act_all] + cot_all, sem)
    lat_cot = jnp.concatenate([l[:, rows:] for l in lats], axis=1)
    for c in made[0]:
        c.wait()
    span = ratio * blk
    for a in range(blocks):
        rws = slice(a * span, (a + 1) * span)
        act_t[rws, :] = act_all[:, rws].T
        gdl[rws, :] = (nt(act_t[rws, :], lat_cot) * scale).astype(BF16)
    for some in made[1:]:
        for c in some:
            c.wait()
    for a in range(blocks):
        lhs = jnp.concatenate(
            [
                act_t[pl.ds(pl.multiple_of((a * ratio + r) * blk + k * part, part), part), :]
                for r in range(ratio)
            ],
            axis=0,
        )
        srcs = [(0, a ^ s) for s in near] + [(1 + j, a) for j in range(n)]
        for j, (i, b) in enumerate(srcs):
            out = nn(lhs, cot_all[i][:, b * blk : (b + 1) * blk]) * scale
            for r in range(ratio):
                gd[a * ratio + r, j] = out[r * part : (r + 1) * part].astype(BF16)


def down_pass(acts, cots, lats, near, part, scale, ratio, blk):
    dp = len(acts)
    n = len(cots) - 1
    rows, hid = acts[0].shape
    width = cots[0][0].shape[1]
    factors = len(near) + n
    vm = pl.BlockSpec(memory_space=pltpu.VMEM)
    anyspec = pl.BlockSpec(memory_space=pl.ANY)
    return pl.pallas_call(
        functools.partial(down_kernel, near, n, dp, ratio, blk, scale),
        in_specs=[anyspec] * (dp * (2 + n)) + [vm] * dp,
        out_specs=[vm, vm],
        out_shape=[
            jax.ShapeDtypeStruct((hid // blk, factors, part, blk), BF16),
            jax.ShapeDtypeStruct((hid, lats[0].shape[0]), BF16),
        ],
        scratch_shapes=[pltpu.VMEM((dp * rows, hid), BF16)]
        + [pltpu.VMEM((dp * rows, width), BF16)] * (1 + n)
        + [pltpu.VMEM((hid, dp * rows), BF16), pltpu.SemaphoreType.DMA((dp * (2 + n),))],
        compiler_params=pltpu.CompilerParams(vmem_limit_bytes=56 * 2**20),
        name="down_pass",
    )(*acts, *[c for some in cots for c in some], *lats)


def up_kernel(near, n_full, n_part, dp, ratio, blk, scale, *refs):
    take = iter(refs)
    toks = [[next(take) for _ in range(dp)] for _ in range(1 + n_full)]
    quarters = [next(take) for _ in range(dp)] if n_part else []
    pres = [next(take) for _ in range(dp)]
    cots = [next(take) for _ in range(dp)]
    lats = [next(take) for _ in range(dp)]
    lats2 = [next(take) for _ in range(dp)]
    gu, gul, gur, gdr = (next(take) for _ in range(4))
    tok_all = [next(take) for _ in range(1 + n_full)]
    q_all = next(take) if n_part else None
    pre_all, cot_all = next(take), next(take)
    tok_t = [next(take) for _ in range(1 + n_full)]
    q_t = next(take) if n_part else None
    sem = next(take)
    rows = lats[0].shape[1] // 2
    blocks = toks[0][0].shape[1] // blk
    part = gu.shape[2]
    k = lax.axis_index("dp")
    groups = toks + ([quarters] if n_part else []) + [cots, pres]
    dsts = tok_all + ([q_all] if n_part else []) + [cot_all, pre_all]
    made = gather_copies(groups, dsts, sem)
    lat_up = jnp.concatenate([l[:, :rows] for l in lats], axis=1)
    lat_down = jnp.concatenate([l[:, :rows] for l in lats2], axis=1)
    lat_pre = jnp.concatenate([l[:, rows:] for l in lats2], axis=1)
    for some in made[:-1]:
        for c in some:
            c.wait()
    for src, dst in zip(tok_all, tok_t):
        dst[...] = src[...].T
    if n_part:
        q_t[...] = q_all[...].T
    gul[...] = (nt(tok_t[0][...], lat_pre) * scale).astype(BF16)
    gdr[...] = (nn(lat_down, cot_all[...]) * scale).astype(BF16)
    for c in made[-1]:
        c.wait()
    span = ratio * blk
    for a in range(blocks):
        pieces = [
            tok_t[0][pl.ds(pl.multiple_of((a ^ s) * blk + k * part, part), part), :] for s in near
        ]
        pieces += [
            tok_t[1 + j][pl.ds(pl.multiple_of(a * blk + k * part, part), part), :]
            for j in range(n_full)
        ]
        pieces += [
            q_t[(j * blocks + a) * part : (j * blocks + a + 1) * part, :] for j in range(n_part)
        ]
        rhs = pre_all[:, a * span : (a + 1) * span]
        out = (nn(jnp.concatenate(pieces, axis=0), rhs) * scale).astype(BF16)
        for r in range(ratio):
            for j in range(len(pieces)):
                gu[a * ratio + r, j] = out[j * part : (j + 1) * part, r * blk : (r + 1) * blk]
        gur[:, a * span : (a + 1) * span] = (nn(lat_up, rhs) * scale).astype(BF16)


def up_pass(toks, quarters, n_part, pres, cots, lats, lats2, near, part, scale, ratio, blk):
    dp = len(pres)
    n_full = len(toks) - 1
    rows, hid = pres[0].shape
    width = toks[0][0].shape[1]
    factors = len(near) + n_full + n_part
    rank_part = lats[0].shape[0]
    vm = pl.BlockSpec(memory_space=pltpu.VMEM)
    anyspec = pl.BlockSpec(memory_space=pl.ANY)
    args = [t for some in toks for t in some] + list(quarters) + list(pres) + list(cots)
    total_rows = dp * rows
    scratch = [pltpu.VMEM((total_rows, width), BF16)] * (1 + n_full)
    if n_part:
        scratch.append(pltpu.VMEM((total_rows, quarters[0].shape[1]), BF16))
    scratch += [pltpu.VMEM((total_rows, hid), BF16), pltpu.VMEM((total_rows, width), BF16)]
    scratch += [pltpu.VMEM((width, total_rows), BF16)] * (1 + n_full)
    if n_part:
        scratch.append(pltpu.VMEM((quarters[0].shape[1], total_rows), BF16))
    scratch.append(pltpu.SemaphoreType.DMA((len(args),)))
    return pl.pallas_call(
        functools.partial(up_kernel, near, n_full, n_part, dp, ratio, blk, scale),
        in_specs=[anyspec] * len(args) + [vm] * (2 * dp),
        out_specs=[vm] * 4,
        out_shape=[
            jax.ShapeDtypeStruct((hid // blk, factors, part, blk), BF16),
            jax.ShapeDtypeStruct((width, rank_part), BF16),
            jax.ShapeDtypeStruct((rank_part, hid), BF16),
            jax.ShapeDtypeStruct((rank_part, width), BF16),
        ],
        scratch_shapes=scratch,
        compiler_params=pltpu.CompilerParams(vmem_limit_bytes=56 * 2**20),
        name="up_pass",
    )(*args, *lats, *lats2)


def shards(tokens, cotangent, up_blocks, down_blocks, up_left, up_right, down_left, down_right):
    rows, width = tokens.shape
    blk = up_blocks.shape[-1]
    blocks = width // blk
    ratio = up_blocks.shape[0] // blocks
    dp = lax.axis_size("dp")
    part, rank_part = blk // dp, up_left.shape[1] // dp
    scale = 1.0 / math.sqrt(rows * dp)
    k = lax.axis_index("dp")
    near = tuple(s for s in STRIDES if s < blocks)
    masks = [s // blocks for s in STRIDES if s >= blocks]
    bits = [1 << b for b in range(dp.bit_length() - 1)]

    def to_group(x, pieces, size):
        out = []
        for m in range(dp):
            piece = lax.dynamic_slice_in_dim(x, (k ^ m) * size, size, axis=0)
            out.append(swapped(piece, "dp", m) if m else piece)
        return out

    tok_far = [swapped(tokens, "tensor", m) for m in masks]
    lat = jnp.concatenate(
        [
            jnp.einsum("td,dr->rt", tokens, up_left, preferred_element_type=F32).astype(BF16),
            jnp.einsum("td,rd->rt", cotangent, down_right, preferred_element_type=F32).astype(BF16),
        ],
        axis=1,
    )
    lat = total(lat)
    cot_far = [swapped(cotangent, "tensor", m) for m in masks]
    tok_groups = spread(tokens, bits)
    cot_groups = spread(cotangent, bits[::-1])

    act, pre, here, *rest = main_pass(
        tokens, cotangent, tok_far, cot_far, lat, up_blocks, down_blocks, up_right, down_left, near
    )
    parts, lat2 = rest[:-1], rest[-1]

    lat_groups = to_group(lat, dp, rank_part)
    full = [i for i, m in enumerate(masks) if m == 1]
    thin = [i for i, m in enumerate(masks) if m != 1]
    tok_lists = [tok_groups] + [
        [tok_far[i]] + [swapped(t, "tensor", masks[i]) for t in tok_groups[1:]] for i in full
    ]
    cot_lists = [cot_groups]
    for i, m in enumerate(masks):
        if m == 1:
            cot_lists.append([cot_far[i]] + [swapped(c, "tensor", m) for c in cot_groups[1:]])
        else:
            cot_lists.append(spread(cot_far[i], bits[::-1] if len(cot_lists) % 2 else bits))
    thin_tok = jnp.concatenate([tok_far[i] for i in thin], axis=1).reshape(
        rows, len(thin) * blocks, dp, part
    )
    quarters = []
    for m in range(dp):
        piece = lax.dynamic_index_in_dim(thin_tok, k ^ m, axis=2, keepdims=False)
        piece = piece.reshape(rows, len(thin) * blocks * part)
        quarters.append(swapped(piece, "dp", m) if m else piece)

    got = [swapped(p, "tensor", m) for p, m in zip(parts, masks)]
    act_groups = spread(act, bits)
    pre_groups = spread(pre, bits[::-1])
    lat2 = total(lat2)
    lat2_groups = to_group(lat2, dp, rank_part)

    gd, gdl = down_pass(act_groups, cot_lists, lat_groups, near, part, scale, ratio, blk)

    summed = here
    for g in got:
        summed = summed + g.astype(F32)
    layer_out = (
        summed[:rows]
        + jnp.einsum("rt,rd->td", lat2[:, :rows], down_right, preferred_element_type=F32)
    ).astype(BF16)
    token_grads = (
        summed[rows:]
        + jnp.einsum("rt,dr->td", lat2[:, rows:], up_left, preferred_element_type=F32)
    ).astype(BF16)

    gu, gul, gur, gdr = up_pass(
        tok_lists, quarters, len(thin), pre_groups, cot_groups, lat_groups, lat2_groups,
        near, part, scale, ratio, blk,
    )
    return layer_out, token_grads, gu, gd, gul, gur, gdl, gdr


def solution(mesh):
    in_specs = (
        P("dp", "tensor"),
        P("dp", "tensor"),
        P("tensor", None, None, None),
        P("tensor", None, None, None),
        P("tensor", None),
        P(None, "tensor"),
        P("tensor", None),
        P(None, "tensor"),
    )
    out_specs = (
        P("dp", "tensor"),
        P("dp", "tensor"),
        P("tensor", None, "dp", None),
        P("tensor", None, "dp", None),
        P("tensor", "dp"),
        P("dp", "tensor"),
        P("tensor", "dp"),
        P("dp", "tensor"),
    )
    return jax.shard_map(shards, mesh=mesh, in_specs=in_specs, out_specs=out_specs, check_vma=False)
```

```python
import functools
import math

import jax
import jax.numpy as jnp
from jax import lax
from jax.experimental import pallas as pl
from jax.experimental.pallas import tpu as pltpu
from jax.sharding import PartitionSpec as P


STRIDES = (0, 1, 2, 4, 8, 16)
ROOT = math.sqrt(2.0 / math.pi)
CUBIC = 0.044715
F32 = jnp.float32
BF16 = jnp.bfloat16


def swapped(x, axis, mask):
    return lax.ppermute(x, axis, [(i, i ^ mask) for i in range(lax.axis_size(axis))])


def spread(x, order):
    got = {0: x}
    for mask in order:
        for m in list(got):
            got[m ^ mask] = swapped(got[m], "dp", mask)
    return [got[m] for m in range(len(got))]


def total(mine, other):
    def add(x, y):
        return (x.astype(F32) + y.astype(F32)).astype(BF16)

    x = add(mine, swapped(other, "tensor", 1))
    mask = lax.axis_size("tensor") // 2
    while mask > 1:
        x = add(x, swapped(x, "tensor", mask))
        mask //= 2
    return x, swapped(x, "tensor", 1)


def nn(a, b):
    return jnp.dot(a, b, preferred_element_type=F32)


def nt(a, b):
    return lax.dot_general(a, b, (((1,), (1,)), ((), ())), preferred_element_type=F32)


def cols(block, blk):
    return pl.ds(pl.multiple_of(block * blk, blk), blk)


def one_hot(rows, width, first):
    r = lax.broadcasted_iota(jnp.int32, (rows, width), 0)
    c = lax.broadcasted_iota(jnp.int32, (rows, width), 1)
    return jnp.where(c == r + first, 1.0, 0.0).astype(BF16)


def params(mib=8):
    return pltpu.CompilerParams(vmem_limit_bytes=mib * 2**20)


VM = pl.BlockSpec(memory_space=pltpu.VMEM)
HBM = pl.BlockSpec(memory_space=pl.ANY)


def halves():
    c = lax.axis_index("tensor") & 1
    return c, 1 - c


def put_halves(dst, mine, other):
    n = mine.shape[0]
    for c, ref in zip(halves(), (mine, other)):
        dst[pl.ds(pl.multiple_of(c * n, n), n), :] = ref[...]


def get_halves(src, mine, other):
    n = mine.shape[0]
    for c, ref in zip(halves(), (mine, other)):
        ref[...] = src[pl.ds(pl.multiple_of(c * n, n), n), :]


def in_hbm(x):
    return pltpu.with_memory_space_constraint(x, pltpu.HBM)


def shape(dims, dtype=BF16):
    return jax.ShapeDtypeStruct(dims, dtype)


class Copies:
    def __init__(self, sem):
        self.sem, self.count, self.out = sem, 0, []

    def start(self, src, dst):
        copy = pltpu.make_async_copy(src, dst, self.sem.at[self.count])
        self.count += 1
        copy.start()
        return copy

    def back(self, src, dst):
        self.out.append(self.start(src, dst))

    def finish(self):
        for copy in self.out:
            copy.wait()


def latent_kernel(tok, cot, ul, dr, mine, other, both, tmp, sem):
    rows = tok.shape[0]
    copies = Copies(sem)
    copies.back(tok, both.at[pl.ds(0, rows), :])
    copies.back(cot, both.at[pl.ds(rows, rows), :])
    tmp[:, :rows] = nn(tok[...], ul[...]).T.astype(BF16)
    tmp[:, rows:] = nt(dr[...], cot[...]).astype(BF16)
    get_halves(tmp, mine, other)
    copies.finish()


def latent_pass(tok, cot, ul, dr):
    rank, (rows, width) = dr.shape[0], tok.shape
    half = shape((rank // 2, 2 * rows))
    return pl.pallas_call(
        latent_kernel,
        in_specs=[VM] * 4,
        out_specs=[VM, VM, HBM],
        out_shape=[half, half, shape((2 * rows, width))],
        scratch_shapes=[pltpu.VMEM((rank, 2 * rows), BF16), pltpu.SemaphoreType.DMA((2,))],
        compiler_params=params(),
        name="kl",
    )(tok, cot, ul, dr)


def join_kernel(*refs):
    both, out, tmp, sem = refs[:-3], refs[-3], refs[-2], refs[-1]
    rows = both[0].shape[0] // 2
    copies = Copies(sem)
    spans = [pl.ds(g * rows, rows) for g in range(len(both))]
    reads = [copies.start(ref.at[pl.ds(rows, rows), :], tmp.at[g, :]) for ref, g in zip(both, spans)]
    for read, g in zip(reads, spans):
        read.wait()
        copies.back(tmp.at[g, :], out.at[g, :])
    copies.finish()


def join_pass(both):
    rows, width = both[0].shape[0] // 2, both[0].shape[1]
    dims = (len(both) * rows, width)
    return pl.pallas_call(
        join_kernel,
        in_specs=[HBM] * len(both),
        out_specs=HBM,
        out_shape=shape(dims),
        scratch_shapes=[pltpu.VMEM(dims, BF16), pltpu.SemaphoreType.DMA((2 * len(both),))],
        compiler_params=params(),
        name="kj",
    )(*both)


def half_kernel(back, near, n, ratio, blk, *refs):
    take = iter(refs)
    x_in = [next(take) for _ in range(1 + n)]
    lat_mine, lat_other, up, down, ur, dl = (next(take) for _ in range(6))
    slope_in, lat_down = (next(take), next(take)) if back else (None, None)
    act_out = next(take)
    slope_out = None if back else next(take)
    here_out = next(take)
    parts_out = [next(take) for _ in range(n)]
    lat_outs = [next(take) for _ in range(2 if back else 1)]
    xs = [next(take) for _ in range(1 + n)]
    lat, up_v, down_v, ur_v, dl_v, slope = (next(take) for _ in range(6))
    act, here = next(take), next(take)
    parts = [next(take) for _ in range(n)]
    lat_tmp, sem = next(take), next(take)
    rows, width = x_in[0].shape
    blocks = width // blk
    half = lat_mine.shape[0]
    copies = Copies(sem)

    def lat_half(src, c):
        return copies.start(src, lat.at[pl.ds(pl.multiple_of(c * half, half), half), :])

    first = [lat_half(src, c) for src, c in zip((lat_mine, lat_other), halves())]
    first += [copies.start(src, dst) for src, dst in zip(x_in, xs)]
    left, right = ((dl, dl_v), (ur, ur_v)) if back else ((ur, ur_v), (dl, dl_v))
    first.append(copies.start(*left))
    one, two = ((down, down_v), (up, up_v)) if back else ((up, up_v), (down, down_v))
    ones, twos = [], []
    for a in range(blocks):
        span = pl.ds(a * ratio, ratio)
        ones.append(copies.start(one[0].at[span], one[1].at[span]))
        if a == 0:
            if back:
                first.append(copies.start(slope_in, slope))
                late = [copies.start(lat_down, lat_tmp)]
            else:
                late = []
            late.append(copies.start(*right))
        twos.append(copies.start(two[0].at[span], two[1].at[span]))
    for copy in first:
        copy.wait()
    lat_t = (lat[:, rows:] if back else lat[:, :rows]).T
    acc = jnp.zeros((rows, dl.shape[1]), F32)
    here[...] = jnp.zeros_like(here)
    for a in range(blocks):
        own = slice(a * blk, (a + 1) * blk)
        at = [slice((a ^ s) * blk, ((a ^ s) + 1) * blk) for s in near]
        pieces = [xs[0][:, c] for c in at] + [x[:, own] for x in xs[1:]]
        ones[a].wait()
        ys = []
        for r in range(ratio):
            h = a * ratio + r
            sl = slice(h * blk, (h + 1) * blk)
            if back:
                g = nt(lat_t, dl_v[sl, :])
                for j, piece in enumerate(pieces):
                    g = g + nt(piece, down_v[h, j])
                y = (g * slope[:, sl]).astype(BF16)
            else:
                v = nn(lat_t, ur_v[:, sl]) + nn(jnp.concatenate(pieces, axis=1), up_v[h].reshape(-1, blk))
                th = jnp.tanh(ROOT * (v + CUBIC * v * v * v))
                y = (0.5 * v * (1.0 + th)).astype(BF16)
                slope[:, sl] = 0.5 * (1.0 + th) + 0.5 * v * (1.0 - th * th) * ROOT * (
                    1.0 + 3.0 * CUBIC * v * v
                )
            act[:, sl] = y
            ys.append(y)
        twos[a].wait()
        if a == 0:
            for copy in late:
                copy.wait()
        for r in range(ratio):
            h = a * ratio + r
            sl = slice(h * blk, (h + 1) * blk)
            acc = acc + (nt(ys[r], ur_v[:, sl]) if back else nn(ys[r], dl_v[sl, :]))
        if a == blocks - 1:
            copies.back(act, act_out)
            if not back:
                copies.back(slope, slope_out)
        for j in list(range(len(near), len(near) + n)) + list(range(len(near))):
            f = sum(
                nt(ys[r], up_v[a * ratio + r, j]) if back else nn(ys[r], down_v[a * ratio + r, j])
                for r in range(ratio)
            )
            if j < len(near):
                here[:, at[j]] += f
            else:
                parts[j - len(near)][:, own] = f.astype(BF16)
        if a == blocks - 1:
            for src, dst in zip(parts, parts_out):
                copies.back(src, dst)
    copies.back(here, here_out)
    if back:
        lat[:, :rows] = lat_tmp[...]
        lat[:, rows:] = acc.T.astype(BF16)
        for dst, c in zip(lat_outs, halves()):
            copies.back(lat.at[pl.ds(pl.multiple_of(c * half, half), half), :], dst)
    else:
        lat_tmp[...] = acc.T.astype(BF16)
        copies.back(lat_tmp, lat_outs[0])
    copies.finish()


def layer_half(x, far, lat, up, down, ur, dl, near, slope=None, lat_down=None):
    back = slope is not None
    rows, width = x.shape
    hidden, _, blk = up.shape[:3]
    blocks = width // blk
    ratio = hidden // blocks
    rank = dl.shape[1]
    n = len(far)
    block, gate, sums = shape((rows, width)), shape((rows, hidden * blk), F32), shape((rows, width), F32)
    wide = shape((rows, hidden * blk))
    outs = [wide] + ([] if back else [gate]) + [sums] + [block] * n
    outs += [shape((rank // 2, 2 * rows))] * 2 if back else [shape((rank, rows))]
    held = [block] * (1 + n) + [shape((rank, 2 * rows))] + [shape(w.shape) for w in (up, down, ur, dl)]
    held += [gate, wide, sums] + [block] * n + [shape((rank, rows))]
    args = [x, *far, *lat, up, down, ur, dl, *((slope, lat_down) if back else ())]
    return pl.pallas_call(
        functools.partial(half_kernel, back, near, n, ratio, blk),
        in_specs=[HBM] * len(args),
        out_specs=[HBM] * len(outs),
        out_shape=outs,
        scratch_shapes=[pltpu.VMEM(h.shape, h.dtype) for h in held]
        + [pltpu.SemaphoreType.DMA((len(args) + len(outs) + 2 * blocks,))],
        compiler_params=params(28),
    )(*args)


def select_kernel(n, dp, part, blk, *refs):
    toks, outs, tmp, sem = refs[:n], refs[n : n + dp], refs[n + dp], refs[n + dp + 1]
    copies = [pltpu.make_async_copy(t, tmp.at[z], sem.at[z]) for z, t in enumerate(toks)]
    for c in copies:
        c.start()
    blocks = tmp.shape[2] // blk
    k = lax.axis_index("dp")
    r = lax.broadcasted_iota(jnp.int32, (blk, blk), 0)
    c = lax.broadcasted_iota(jnp.int32, (blk, blk), 1)
    pick = jnp.where(c == jnp.bitwise_xor(r, k * part), 1.0, 0.0).astype(BF16)
    for z in range(n):
        copies[z].wait()
        for b in range(blocks):
            at = (z * blocks + b) * part
            out = nt(pick, tmp[z, :, b * blk : (b + 1) * blk]).astype(BF16)
            for m in range(dp):
                outs[m][at : at + part, :] = out[m * part : (m + 1) * part]


def select_pass(toks, dp, part, blk):
    rows, width = toks[0].shape
    n = len(toks)
    return pl.pallas_call(
        functools.partial(select_kernel, n, dp, part, blk),
        in_specs=[HBM] * n,
        out_specs=[VM] * dp,
        out_shape=[shape((n * (width // blk) * part, rows))] * dp,
        scratch_shapes=[pltpu.VMEM((n, rows, width), BF16), pltpu.SemaphoreType.DMA((n,))],
        compiler_params=params(),
        name="ks",
    )(*toks)


def cut_kernel(dp, rank_part, *refs):
    first, second = refs[:2], refs[2:4]
    outs, whole2, whole1 = refs[4 : 4 + dp], refs[4 + dp], refs[5 + dp]
    put_halves(whole1, *first)
    put_halves(whole2, *second)
    k = lax.axis_index("dp")
    for m in range(dp):
        rows = cols(jnp.bitwise_xor(k, m), rank_part)
        outs[m][:rank_part, :] = whole1[rows, :]
        outs[m][rank_part:, :] = whole2[rows, :]


def cut_pass(first, second, dp, rank_part):
    rank, count = 2 * first[0].shape[0], first[0].shape[1]
    return pl.pallas_call(
        functools.partial(cut_kernel, dp, rank_part),
        in_specs=[VM] * 4,
        out_specs=[VM] * (dp + 1),
        out_shape=[shape((2 * rank_part, count))] * dp + [shape((rank, count))],
        scratch_shapes=[pltpu.VMEM((rank, count), BF16)],
        compiler_params=params(),
        name="kc",
    )(*first, *second)


def gather_copies(groups, scratch, sem):
    made, at = [], 0
    for refs, dst in zip(groups, scratch):
        rows = refs[0].shape[0]
        some = []
        for m, ref in enumerate(refs):
            some.append(pltpu.make_async_copy(ref, dst.at[pl.ds(m * rows, rows), :], sem.at[at]))
            at += 1
        made.append(some)
    for some in made:
        for c in some:
            c.start()
    return made


def wait_all(some):
    for c in some:
        c.wait()


def split_groups(first, both, base):
    rows = first.shape[0]
    return [first] + [ref.at[pl.ds(base * rows, rows), :] for ref in both]


def down_kernel(near, kinds, dp, ratio, blk, scale, *refs):
    take = iter(refs)
    tok, cot = next(take), next(take)
    both = [next(take) for _ in range(dp - 1)]
    rows, width = tok.shape
    cots = [split_groups(cot, both, 1)]
    for joint in kinds:
        if joint:
            far, rest = next(take), next(take)
            cots.append([far] + [rest.at[pl.ds(g * rows, rows), :] for g in range(dp - 1)])
        else:
            cots.append([next(take) for _ in range(dp)])
    acts = [next(take) for _ in range(dp)]
    gd, own_rows = next(take), next(take)
    tok_all = next(take)
    cot_all = [next(take) for _ in cots]
    act_all = next(take)
    made = gather_copies([split_groups(tok, both, 0)] + cots + [acts], [tok_all] + cot_all + [act_all], next(take))
    blocks = width // blk
    part = gd.shape[2]
    pick = one_hot(part, blk, lax.axis_index("dp") * part)
    wait_all(made[0])
    for b in range(blocks):
        own_rows[b * part : (b + 1) * part, :] = nt(pick, tok_all[:, b * blk : (b + 1) * blk]).astype(BF16)
    for some in made[1:]:
        wait_all(some)
    for a in range(blocks):
        lhs = jnp.concatenate(
            [
                nt(pick, act_all[:, (a * ratio + r) * blk : (a * ratio + r + 1) * blk]).astype(BF16)
                for r in range(ratio)
            ],
            axis=0,
        )
        srcs = [(0, a ^ s) for s in near] + [(1 + j, a) for j in range(len(kinds))]
        for j, (i, b) in enumerate(srcs):
            out = (nn(lhs, cot_all[i][:, b * blk : (b + 1) * blk]) * scale).astype(BF16)
            for r in range(ratio):
                gd[a * ratio + r, j] = out[r * part : (r + 1) * part]


def stacked(dims, count):
    return [pltpu.VMEM(d, t) for d, t in dims] + [pltpu.SemaphoreType.DMA((count,))]


def down_pass(tok, cot, both, far, acts, near, part, scale, blk):
    dp = len(acts)
    rows, width = tok.shape
    hid = acts[0].shape[1]
    kinds = tuple(len(f) == 2 for f in far)
    args = [tok, cot, *both, *[x for f in far for x in f], *acts]
    dims = [((dp * rows, width), BF16)] * (2 + len(far)) + [((dp * rows, hid), BF16)]
    return pl.pallas_call(
        functools.partial(down_kernel, near, kinds, dp, hid // width, blk, scale),
        in_specs=[HBM] * len(args),
        out_specs=[VM] * 2,
        out_shape=[shape((hid // blk, len(near) + len(far), part, blk)), shape((width // blk * part, dp * rows))],
        scratch_shapes=stacked(dims, dp * len(dims)),
        compiler_params=params(24),
        name="kd",
    )(*args)


def rank_kernel(n, dp, rank_part, scale, *refs):
    take = iter(refs)
    tok, cot = next(take), next(take)
    both = [next(take) for _ in range(dp - 1)]
    acts, lats = ([next(take) for _ in range(dp)] for _ in range(2))
    singles = [[next(take)] for _ in range(5 + 2 * n)]
    gdl, gul, gdr, layer_out, token_grads = (next(take) for _ in range(5))
    groups = [acts, split_groups(tok, both, 0), split_groups(cot, both, 1), lats] + singles
    scratch = [next(take) for _ in groups]
    made = gather_copies(groups, scratch, next(take))
    act_all, tok_all, cot_all, lat_all, out_here, grad_here, dr, ul, lat2 = scratch[:9]
    rows, _ = tok.shape
    for some in made:
        wait_all(some)

    def lat_rows(second, half):
        piece = lat_all.at[:, half * rows : (half + 1) * rows]
        first = rank_part if second else 0
        return jnp.concatenate(
            [piece[2 * rank_part * m + first : 2 * rank_part * m + first + rank_part, :] for m in range(dp)],
            axis=1,
        )

    gdl[...] = (nn(lat_rows(False, 1), act_all[...]) * scale).astype(BF16)
    gdr[...] = (nn(lat_rows(True, 0), cot_all[...]) * scale).astype(BF16)
    gul[...] = (nn(lat_rows(True, 1), tok_all[...]) * scale).astype(BF16)
    out = out_here[...] + nn(lat2[:, :rows].T, dr[...])
    grad = grad_here[...] + nt(lat2[:, rows:].T, ul[...])
    for p, q in zip(scratch[9 : 9 + n], scratch[9 + n :]):
        out = out + p[...].astype(F32)
        grad = grad + q[...].astype(F32)
    layer_out[...] = out.astype(BF16)
    token_grads[...] = grad.astype(BF16)


def rank_pass(tok, cot, both, acts, lats, singles, n, rank_part, scale):
    dp = len(acts)
    rows, width = tok.shape
    hid = acts[0].shape[1]
    args = [tok, cot, *both, *acts, *lats, *singles]
    dims = [((dp * rows, hid), BF16)] + [((dp * rows, width), BF16)] * 2
    dims += [((dp * lats[0].shape[0], lats[0].shape[1]), BF16)] + [(x.shape, x.dtype) for x in singles]
    wide, full = shape((rank_part, width)), shape((rows, width))
    return pl.pallas_call(
        functools.partial(rank_kernel, n, dp, rank_part, scale),
        in_specs=[HBM] * len(args),
        out_specs=[VM] * 5,
        out_shape=[shape((rank_part, hid)), wide, wide, full, full],
        scratch_shapes=stacked(dims, 4 * dp + len(singles)),
        compiler_params=params(16),
        name="kr",
    )(*args)


def up_kernel(near, n_full, n_thin, dp, ratio, blk, rank_part, scale, *refs):
    take = iter(refs)
    pres = [next(take) for _ in range(dp)]
    lats = [next(take) for _ in range(dp)]
    thin = [next(take) for _ in range(dp)] if n_thin else []
    full = [[next(take)] for _ in range(1 + n_full)]
    gu, gur = next(take), next(take)
    groups = [lats] + ([thin] if n_thin else []) + full + [pres]
    scratch = [next(take) for _ in groups]
    lhs_all, sem = next(take), next(take)
    made = gather_copies(groups, scratch, sem)
    part = gu.shape[2]
    rows = pres[0].shape[0]
    lat_all, pre_all = scratch[0], scratch[-1]
    full_all = scratch[-2 - n_full : -1]
    blocks = full_all[0].shape[0] // part
    count = len(near) + n_full + n_thin
    step = count * part + rank_part
    for some in made[:-1]:
        wait_all(some)
    for a in range(blocks):
        pieces = [full_all[0][(a ^ s) * part : ((a ^ s) + 1) * part, :] for s in near]
        pieces += [f[a * part : (a + 1) * part, :] for f in full_all[1:]]
        for j in range(n_thin):
            at = (j * blocks + a) * part
            tall = thin[0].shape[0]
            pieces.append(
                jnp.concatenate([scratch[1][m * tall + at : m * tall + at + part, :] for m in range(dp)], axis=1)
            )
        pieces.append(
            jnp.concatenate(
                [lat_all[2 * rank_part * m : 2 * rank_part * m + rank_part, :rows] for m in range(dp)], axis=1
            )
        )
        lhs_all[a * step : (a + 1) * step, :] = jnp.concatenate(pieces, axis=0)
    wait_all(made[-1])
    for a in range(blocks):
        for r in range(ratio):
            h = a * ratio + r
            out = nn(lhs_all[a * step : (a + 1) * step, :], pre_all[:, h * blk : (h + 1) * blk])
            out = (out * scale).astype(BF16)
            for j in range(count):
                gu[h, j] = out[j * part : (j + 1) * part]
            gur[:, h * blk : (h + 1) * blk] = out[count * part :]


def up_pass(pres, lats, thin, n_thin, full, near, part, rank_part, scale, blk):
    dp = len(pres)
    rows, hid = pres[0].shape
    count = len(near) + len(full) - 1 + n_thin
    thin = list(thin) if n_thin else []
    args = [*pres, *lats, *thin, *full]
    blocks = full[0].shape[0] // part
    groups = [lats] + ([thin] if n_thin else []) + [[f] for f in full] + [pres]
    dims = [((len(g) * g[0].shape[0], g[0].shape[1]), BF16) for g in groups]
    dims.append(((blocks * (count * part + rank_part), dp * rows), BF16))
    return pl.pallas_call(
        functools.partial(up_kernel, near, len(full) - 1, n_thin, dp, hid // (blocks * blk), blk, rank_part, scale),
        in_specs=[HBM] * len(args),
        out_specs=[VM, VM],
        out_shape=[shape((hid // blk, count, part, blk)), shape((rank_part, hid))],
        scratch_shapes=stacked(dims, len(args)),
        compiler_params=params(20),
        name="ku",
    )(*args)


def shards(tokens, cotangent, up_blocks, down_blocks, up_left, up_right, down_left, down_right):
    rows, width = tokens.shape
    blk = up_blocks.shape[-1]
    blocks = width // blk
    dp = lax.axis_size("dp")
    part, rank_part = blk // dp, up_left.shape[1] // dp
    scale = 1.0 / math.sqrt(rows * dp)
    near = tuple(s for s in STRIDES if s < blocks)
    masks = [s // blocks for s in STRIDES if s >= blocks]
    bits = [1 << b for b in range(dp.bit_length() - 1)]
    flip = bits[::-1]
    thin = [i for i, m in enumerate(masks) if m != 1]
    n = len(masks)
    tokens, cotangent, up_blocks, down_blocks = (in_hbm(x) for x in (tokens, cotangent, up_blocks, down_blocks))
    up_left, up_right, down_left, down_right = (in_hbm(x) for x in (up_left, up_right, down_left, down_right))

    tok_far = [swapped(tokens, "tensor", m) for m in masks]
    cot_far = [swapped(cotangent, "tensor", m) for m in masks]
    *lat_parts, both = latent_pass(tokens, cotangent, up_left, down_right)
    both = spread(both, bits)[1:]
    lat = total(*lat_parts)
    sent = select_pass([tok_far[i] for i in thin], dp, part, blk) if thin else []
    thin_groups = [swapped(x, "dp", m) if m else x for m, x in enumerate(sent)]
    others = join_pass(both)
    far = [
        (cot_far[i], swapped(others, "tensor", m)) if m <= 2 else spread(cot_far[i], flip)
        for i, m in enumerate(masks)
    ]

    weights = (up_blocks, down_blocks, up_right, down_left)
    made = layer_half(tokens, tok_far, lat, *weights, near)
    act, slope, out_here, *out_parts, lat_down = made
    made = layer_half(cotangent, cot_far, lat, *weights, near, slope, lat_down)
    pre, grad_here, *grad_parts, lat_mine, lat_other = made
    out_parts = [swapped(x, "tensor", m) for x, m in zip(out_parts, masks)]
    grad_parts = [swapped(x, "tensor", m) for x, m in zip(grad_parts, masks)]
    act_groups = spread(act, bits)
    pre_groups = spread(pre, flip)
    *pieces, lat2 = cut_pass(lat, total(lat_mine, lat_other), dp, rank_part)
    lat_groups = [swapped(x, "dp", m) if m else x for m, x in enumerate(pieces)]

    gd, own_rows = down_pass(tokens, cotangent, both, far, act_groups, near, part, scale, blk)
    gdl, gul, gdr, layer_out, token_grads = rank_pass(
        tokens, cotangent, both, act_groups, lat_groups,
        [out_here, grad_here, down_right, up_left, lat2, *out_parts, *grad_parts], n, rank_part, scale,
    )
    full_rows = [own_rows] + [swapped(own_rows, "tensor", m) for m in masks if m == 1]
    gu, gur = up_pass(
        pre_groups, lat_groups, thin_groups, len(thin), full_rows, near, part, rank_part, scale, blk
    )
    return layer_out, token_grads, gu, gd, gul.T, gur, gdl.T, gdr


def solution(mesh):
    d, t = "dp", "tensor"
    blocks = P(t, None, None, None)
    in_specs = (P(d, t), P(d, t), blocks, blocks, P(t, None), P(None, t), P(t, None), P(None, t))
    cut = P(t, None, d, None)
    out_specs = (P(d, t), P(d, t), cut, cut, P(t, d), P(d, t), P(t, d), P(d, t))
    return jax.shard_map(shards, mesh=mesh, in_specs=in_specs, out_specs=out_specs, check_vma=False)
```

```python
import functools
import math

import jax
import jax.numpy as jnp
from jax import lax
from jax.experimental import pallas as pl
from jax.experimental.pallas import tpu as pltpu
from jax.sharding import PartitionSpec as P


STRIDES = (0, 1, 2, 4, 8, 16)
ROOT = math.sqrt(2.0 / math.pi)
CUBIC = 0.044715
F32 = jnp.float32
BF16 = jnp.bfloat16


def swapped(x, axis, mask):
    return lax.ppermute(x, axis, [(i, i ^ mask) for i in range(lax.axis_size(axis))])


def spread(x, order):
    got = {0: x}
    for mask in order:
        for m in list(got):
            got[m ^ mask] = swapped(got[m], "dp", mask)
    return [got[m] for m in range(len(got))]


def exchange(pieces):
    return [swapped(x, "dp", m) if m else x for m, x in enumerate(pieces)]


def total(mine, other):
    def add(x, y):
        return (x.astype(F32) + y.astype(F32)).astype(BF16)

    x = add(mine, swapped(other, "tensor", 1))
    mask = lax.axis_size("tensor") // 2
    while mask > 1:
        x = add(x, swapped(x, "tensor", mask))
        mask //= 2
    return x, swapped(x, "tensor", 1)


def nn(a, b):
    return jnp.dot(a, b, preferred_element_type=F32)


def nt(a, b):
    return lax.dot_general(a, b, (((1,), (1,)), ((), ())), preferred_element_type=F32)


def cols(block, blk):
    return pl.ds(pl.multiple_of(block * blk, blk), blk)


def one_hot(rows, width, first):
    r = lax.broadcasted_iota(jnp.int32, (rows, width), 0)
    c = lax.broadcasted_iota(jnp.int32, (rows, width), 1)
    return jnp.where(c == r + first, 1.0, 0.0).astype(BF16)


def params(mib=8):
    return pltpu.CompilerParams(vmem_limit_bytes=mib * 2**20)


VM = pl.BlockSpec(memory_space=pltpu.VMEM)
HBM = pl.BlockSpec(memory_space=pl.ANY)


def halves():
    c = lax.axis_index("tensor") & 1
    return c, 1 - c


def put_halves(dst, mine, other):
    n = mine.shape[0]
    for c, ref in zip(halves(), (mine, other)):
        dst[pl.ds(pl.multiple_of(c * n, n), n), :] = ref[...]


def get_halves(src, mine, other):
    n = mine.shape[0]
    for c, ref in zip(halves(), (mine, other)):
        ref[...] = src[pl.ds(pl.multiple_of(c * n, n), n), :]


def in_hbm(x):
    return pltpu.with_memory_space_constraint(x, pltpu.HBM)


def shape(dims, dtype=BF16):
    return jax.ShapeDtypeStruct(dims, dtype)


class Copies:
    def __init__(self, sem):
        self.sem, self.count, self.out = sem, 0, []

    def start(self, src, dst):
        copy = pltpu.make_async_copy(src, dst, self.sem.at[self.count])
        self.count += 1
        copy.start()
        return copy

    def back(self, src, dst):
        self.out.append(self.start(src, dst))

    def finish(self):
        for copy in self.out:
            copy.wait()


def latent_kernel(tok, cot, ul, dr, mine, other, both, tmp, sem):
    rows = tok.shape[0]
    copies = Copies(sem)
    copies.back(tok, both.at[pl.ds(0, rows), :])
    copies.back(cot, both.at[pl.ds(rows, rows), :])
    tmp[:, :rows] = nn(tok[...], ul[...]).T.astype(BF16)
    tmp[:, rows:] = nt(dr[...], cot[...]).astype(BF16)
    get_halves(tmp, mine, other)
    copies.finish()


def latent_pass(tok, cot, ul, dr):
    rank, (rows, width) = dr.shape[0], tok.shape
    half = shape((rank // 2, 2 * rows))
    return pl.pallas_call(
        latent_kernel,
        in_specs=[VM] * 4,
        out_specs=[VM, VM, HBM],
        out_shape=[half, half, shape((2 * rows, width))],
        scratch_shapes=[pltpu.VMEM((rank, 2 * rows), BF16), pltpu.SemaphoreType.DMA((2,))],
        compiler_params=params(),
        name="kl",
    )(tok, cot, ul, dr)


def join_kernel(*refs):
    both, out, tmp, sem = refs[:-3], refs[-3], refs[-2], refs[-1]
    rows = both[0].shape[0] // 2
    copies = Copies(sem)
    spans = [pl.ds(g * rows, rows) for g in range(len(both))]
    reads = [copies.start(ref.at[pl.ds(rows, rows), :], tmp.at[g, :]) for ref, g in zip(both, spans)]
    for read, g in zip(reads, spans):
        read.wait()
        copies.back(tmp.at[g, :], out.at[g, :])
    copies.finish()


def join_pass(both):
    rows, width = both[0].shape[0] // 2, both[0].shape[1]
    dims = (len(both) * rows, width)
    return pl.pallas_call(
        join_kernel,
        in_specs=[HBM] * len(both),
        out_specs=HBM,
        out_shape=shape(dims),
        scratch_shapes=[pltpu.VMEM(dims, BF16), pltpu.SemaphoreType.DMA((2 * len(both),))],
        compiler_params=params(),
        name="kj",
    )(*both)


def half_kernel(back, near, thin, n, dp, ratio, blk, *refs):
    take = iter(refs)
    x_in = [next(take) for _ in range(1 + n)]
    lat_mine, lat_other, up, down, ur, dl = (next(take) for _ in range(6))
    slope_in, lat_down = (next(take), next(take)) if back else (None, None)
    act_outs = [next(take) for _ in range(1 if back else dp)]
    slope_out = None if back else next(take)
    here_out = next(take)
    parts_out = [next(take) for _ in range(n)]
    lat_outs = [next(take) for _ in range(2 if back else 1)]
    xs = [next(take) for _ in range(1 + n)]
    lat, up_v, down_v, ur_v, dl_v, slope = (next(take) for _ in range(6))
    act, here = next(take), next(take)
    parts = [next(take) for _ in range(n)]
    lat_tmp = next(take)
    lat_slabs = None if back else next(take)
    sem = next(take)
    rows, width = x_in[0].shape
    blocks = width // blk
    half = lat_mine.shape[0]
    copies = Copies(sem)

    def lat_half(src, c):
        return copies.start(src, lat.at[pl.ds(pl.multiple_of(c * half, half), half), :])

    first = [lat_half(src, c) for src, c in zip((lat_mine, lat_other), halves())]
    first += [copies.start(src, dst) for src, dst in zip(x_in, xs)]
    left, right = ((dl, dl_v), (ur, ur_v)) if back else ((ur, ur_v), (dl, dl_v))
    first.append(copies.start(*left))
    one, two = ((down, down_v), (up, up_v)) if back else ((up, up_v), (down, down_v))
    ones, twos = [], []
    for a in range(blocks):
        span = pl.ds(a * ratio, ratio)
        ones.append(copies.start(one[0].at[span], one[1].at[span]))
        if a == 0:
            if back:
                first.append(copies.start(slope_in, slope))
                late = [copies.start(lat_down, lat_tmp)]
            else:
                late = []
            late.append(copies.start(*right))
        twos.append(copies.start(two[0].at[span], two[1].at[span]))
    part = blk // dp
    hidden = blocks * ratio
    for copy in first:
        copy.wait()
    if not back:
        for q in range(2 * dp):
            side, m = divmod(q, dp)
            lat_slabs[q] = lat[m * part : (m + 1) * part, side * rows : (side + 1) * rows]
        for z, i in enumerate(thin):
            for b in range(blocks):
                act[hidden + z * blocks + b] = xs[1 + i][:, b * blk : (b + 1) * blk].T
    lat_t = (lat[:, rows:] if back else lat[:, :rows]).T
    acc = jnp.zeros((rows, dl.shape[1]), F32)
    here[...] = jnp.zeros_like(here)
    for a in range(blocks):
        own = slice(a * blk, (a + 1) * blk)
        at = [slice((a ^ s) * blk, ((a ^ s) + 1) * blk) for s in near]
        pieces = [xs[0][:, c] for c in at] + [x[:, own] for x in xs[1:]]
        ones[a].wait()
        ys = []
        for r in range(ratio):
            h = a * ratio + r
            sl = slice(h * blk, (h + 1) * blk)
            if back:
                g = nt(lat_t, dl_v[sl, :])
                for j, piece in enumerate(pieces):
                    g = g + nt(piece, down_v[h, j])
                y = (g * slope[:, sl]).astype(BF16)
            else:
                v = nn(lat_t, ur_v[:, sl]) + nn(jnp.concatenate(pieces, axis=1), up_v[h].reshape(-1, blk))
                th = jnp.tanh(ROOT * (v + CUBIC * v * v * v))
                y = (0.5 * v * (1.0 + th)).astype(BF16)
                slope[:, sl] = 0.5 * (1.0 + th) + 0.5 * v * (1.0 - th * th) * ROOT * (
                    1.0 + 3.0 * CUBIC * v * v
                )
            if back:
                act[:, sl] = y
            else:
                act[h] = y.T
            ys.append(y)
        twos[a].wait()
        if a == 0:
            for copy in late:
                copy.wait()
        for r in range(ratio):
            h = a * ratio + r
            sl = slice(h * blk, (h + 1) * blk)
            acc = acc + (nt(ys[r], ur_v[:, sl]) if back else nn(ys[r], dl_v[sl, :]))
        if a == blocks - 1:
            if back:
                copies.back(act, act_outs[0])
            else:
                k, top = lax.axis_index("dp"), act.shape[0]
                for m, dst in enumerate(act_outs):
                    to = jnp.bitwise_xor(k, m)
                    copies.back(act.at[:, cols(to, part), :], dst.at[pl.ds(0, top)])
                    copies.back(lat_slabs.at[pl.ds(dp, dp)], dst.at[pl.ds(top, dp)])
                    copies.back(lat_slabs.at[to], dst.at[top + dp])
                copies.back(slope, slope_out)
        for j in list(range(len(near), len(near) + n)) + list(range(len(near))):
            f = sum(
                nt(ys[r], up_v[a * ratio + r, j]) if back else nn(ys[r], down_v[a * ratio + r, j])
                for r in range(ratio)
            )
            if j < len(near):
                here[:, at[j]] += f
            else:
                parts[j - len(near)][:, own] = f.astype(BF16)
        if a == blocks - 1:
            for src, dst in zip(parts, parts_out):
                copies.back(src, dst)
    copies.back(here, here_out)
    if back:
        lat[:, :rows] = lat_tmp[...]
        lat[:, rows:] = acc.T.astype(BF16)
        for dst, c in zip(lat_outs, halves()):
            copies.back(lat.at[pl.ds(pl.multiple_of(c * half, half), half), :], dst)
    else:
        lat_tmp[...] = acc.T.astype(BF16)
        copies.back(lat_tmp, lat_outs[0])
    copies.finish()


def layer_half(dp, thin, x, far, lat, up, down, ur, dl, near, slope=None, lat_down=None):
    back = slope is not None
    rows, width = x.shape
    hidden, _, blk = up.shape[:3]
    blocks = width // blk
    ratio = hidden // blocks
    rank = dl.shape[1]
    n = len(far)
    block, gate, sums = shape((rows, width)), shape((rows, hidden * blk), F32), shape((rows, width), F32)
    tall, part = hidden + len(thin) * blocks, blk // dp
    wide = [shape((rows, hidden * blk))] if back else [shape((tall + dp + 1, part, rows))] * dp
    outs = wide + ([] if back else [gate]) + [sums] + [block] * n
    outs += [shape((rank // 2, 2 * rows))] * 2 if back else [shape((rank, rows))]
    held = [block] * (1 + n) + [shape((rank, 2 * rows))] + [shape(w.shape) for w in (up, down, ur, dl)]
    held += [gate, wide[0] if back else shape((tall, blk, rows)), sums] + [block] * n + [shape((rank, rows))] + ([] if back else [shape((2 * dp, part, rows))])
    args = [x, *far, *lat, up, down, ur, dl, *((slope, lat_down) if back else ())]
    return pl.pallas_call(
        functools.partial(half_kernel, back, near, thin, n, dp, ratio, blk),
        in_specs=[HBM] * len(args),
        out_specs=[HBM] * len(outs),
        out_shape=outs,
        scratch_shapes=[pltpu.VMEM(h.shape, h.dtype) for h in held]
        + [pltpu.SemaphoreType.DMA((len(args) + len(outs) + 2 * blocks + 2 * dp,))],
        compiler_params=params(28),
    )(*args)


def cut_kernel(dp, rank_part, mine, other, *outs):
    whole = outs[dp]
    put_halves(whole, mine, other)
    k = lax.axis_index("dp")
    for m in range(dp):
        outs[m][...] = whole[cols(jnp.bitwise_xor(k, m), rank_part), :]


def cut_pass(lat, dp, rank_part):
    rank, count = 2 * lat[0].shape[0], lat[0].shape[1]
    return pl.pallas_call(
        functools.partial(cut_kernel, dp, rank_part),
        in_specs=[VM] * 2,
        out_specs=[VM] * (dp + 1),
        out_shape=[shape((rank_part, count))] * dp + [shape((rank, count))],
        compiler_params=params(),
        name="kc",
    )(*lat)


def gather_copies(groups, scratch, sem):
    copies = Copies(sem)
    made = []
    for refs, dst in zip(groups, scratch):
        rows, width = refs[0].shape
        side = dst.shape[0] == rows
        made.append(
            [
                copies.start(
                    ref, dst.at[:, pl.ds(m * width, width)] if side else dst.at[pl.ds(m * rows, rows), :]
                )
                for m, ref in enumerate(refs)
            ]
        )
    return made


def wait_all(some):
    for c in some:
        c.wait()


def split_groups(first, both, base):
    rows = first.shape[0]
    return [first] + [ref.at[pl.ds(base * rows, rows), :] for ref in both]


def down_kernel(near, kinds, dp, ratio, blk, rank_part, scale, *refs):
    take = iter(refs)
    tok, cot = next(take), next(take)
    both = [next(take) for _ in range(dp - 1)]
    rows, width = tok.shape
    cots = [split_groups(cot, both, 1)]
    for joint in kinds:
        if joint:
            far, rest = next(take), next(take)
            cots.append([far] + [rest.at[pl.ds(g * rows, rows), :] for g in range(dp - 1)])
        else:
            cots.append([next(take) for _ in range(dp)])
    acts = [next(take) for _ in range(dp)]
    lats = [next(take) for _ in range(dp)]
    gd, own_rows, gul, gdr = (next(take) for _ in range(4))
    gdl = [next(take) for _ in range(dp)]
    tok_all = next(take)
    cot_all = [next(take) for _ in cots]
    act_all, lat_all, gdl_all = (next(take) for _ in range(3))
    made = gather_copies(
        [split_groups(tok, both, 0), acts] + cots + [lats], [tok_all, act_all] + cot_all + [lat_all], next(take)
    )
    blocks = width // blk
    hidden, part = gd.shape[0], gd.shape[2]
    rank = dp * rank_part
    k = lax.axis_index("dp")
    pick = one_hot(part, blk, k * part)
    wait_all(made[0])
    for b in range(blocks):
        own_rows[b * part : (b + 1) * part, :] = nt(pick, tok_all[:, b * blk : (b + 1) * blk]).astype(BF16)
    wait_all(made[1])
    lat_cot = act_all[act_all.shape[0] - rank - rank_part : act_all.shape[0] - rank_part, :]
    gdl_all[...] = (nt(lat_cot, act_all[: hidden * part, :]) * scale).astype(BF16)
    for m in range(dp):
        gdl[m][...] = gdl_all[cols(jnp.bitwise_xor(k, m), rank_part), :]
    for some in made[2:]:
        wait_all(some)

    def lat_rows(half):
        return jnp.concatenate(
            [
                lat_all[m * rank_part : (m + 1) * rank_part, half * rows : (half + 1) * rows]
                for m in range(dp)
            ],
            axis=1,
        )

    gdr[...] = (nn(lat_rows(0), cot_all[0][...]) * scale).astype(BF16)
    gul[...] = (nn(lat_rows(1), tok_all[...]) * scale).astype(BF16)
    for a in range(blocks):
        lhs = act_all[a * ratio * part : (a + 1) * ratio * part, :]
        srcs = [(0, a ^ s) for s in near] + [(1 + j, a) for j in range(len(kinds))]
        for j, (i, b) in enumerate(srcs):
            out = (nn(lhs, cot_all[i][:, b * blk : (b + 1) * blk]) * scale).astype(BF16)
            for r in range(ratio):
                gd[a * ratio + r, j] = out[r * part : (r + 1) * part]


def stacked(dims, count):
    return [pltpu.VMEM(d, t) for d, t in dims] + [pltpu.SemaphoreType.DMA((count,))]


def down_pass(tok, cot, both, far, acts, lats, hidden, near, part, scale, blk):
    dp = len(acts)
    rows, width = tok.shape
    rank_part = lats[0].shape[0]
    count = hidden * part
    kinds = tuple(len(f) == 2 for f in far)
    args = [tok, cot, *both, *[x for f in far for x in f], *acts, *lats]
    dims = [((dp * rows, width), BF16), ((acts[0].shape[0], dp * rows), BF16)]
    dims = dims[:1] + [((dp * rows, width), BF16)] * (1 + len(far)) + dims[1:]
    dims += [((dp * rank_part, 2 * rows), BF16), ((dp * rank_part, count), BF16)]
    wide = shape((rank_part, width))
    return pl.pallas_call(
        functools.partial(down_kernel, near, kinds, dp, hidden * blk // width, blk, rank_part, scale),
        in_specs=[HBM] * len(args),
        out_specs=[VM] * (4 + dp),
        out_shape=[
            shape((hidden, len(near) + len(far), part, blk)),
            shape((width // blk * part, dp * rows)),
            wide,
            wide,
        ]
        + [shape((rank_part, count))] * dp,
        scratch_shapes=stacked(dims, dp * (len(dims) - 1)),
        compiler_params=params(24),
        name="kd",
    )(*args)


def rank_kernel(n, dp, blk, *refs):
    take = iter(refs)
    pieces = [next(take) for _ in range(dp)]
    singles = [[next(take)] for _ in range(5 + 2 * n)]
    gdl, layer_out, token_grads = (next(take) for _ in range(3))
    groups = [pieces] + singles
    scratch = [next(take) for _ in groups]
    made = gather_copies(groups, scratch, next(take))
    gdl_all, out_here, grad_here, dr, ul, lat2 = scratch[:6]
    rows = out_here.shape[0]
    part = blk // dp
    rank_part, count = pieces[0].shape
    some = min(count, max(128, part))
    each = some // part * blk
    r = lax.broadcasted_iota(jnp.int32, (some, each), 0)
    c = lax.broadcasted_iota(jnp.int32, (some, each), 1)
    places = [
        jnp.where(
            c == r // part * blk + jnp.bitwise_xor(lax.axis_index("dp"), m) * part + r % part, 1.0, 0.0
        ).astype(BF16)
        for m in range(dp)
    ]
    wait_all(made[0])
    for g in range(count // some):
        out = sum(
            nn(gdl_all[m * rank_part : (m + 1) * rank_part, g * some : (g + 1) * some], places[m])
            for m in range(dp)
        )
        gdl[:, g * each : (g + 1) * each] = out.astype(BF16)
    for some in made[1:]:
        wait_all(some)
    out = out_here[...] + nn(lat2[:, :rows].T, dr[...])
    grad = grad_here[...] + nt(lat2[:, rows:].T, ul[...])
    for p, q in zip(scratch[6 : 6 + n], scratch[6 + n :]):
        out = out + p[...].astype(F32)
        grad = grad + q[...].astype(F32)
    layer_out[...] = out.astype(BF16)
    token_grads[...] = grad.astype(BF16)


def rank_pass(pieces, singles, n, blk):
    dp = len(pieces)
    rank_part, count = pieces[0].shape
    args = [*pieces, *singles]
    dims = [((dp * rank_part, count), BF16)] + [(x.shape, x.dtype) for x in singles]
    full = shape(singles[0].shape)
    return pl.pallas_call(
        functools.partial(rank_kernel, n, dp, blk),
        in_specs=[HBM] * len(args),
        out_specs=[VM] * 3,
        out_shape=[shape((rank_part, count * dp)), full, full],
        scratch_shapes=stacked(dims, len(args)),
        compiler_params=params(16),
        name="kr",
    )(*args)


def up_kernel(near, n_full, n_thin, first, dp, ratio, blk, rank_part, scale, *refs):
    take = iter(refs)
    pres, acts = ([next(take) for _ in range(dp)] for _ in range(2))
    full = [[next(take)] for _ in range(1 + n_full)]
    gu, gur = next(take), next(take)
    groups = [acts] + full + [pres]
    scratch = [next(take) for _ in groups]
    lhs_all, sem = next(take), next(take)
    made = gather_copies(groups, scratch, sem)
    part = gu.shape[2]
    act_all, full_all, pre_all = scratch[0], scratch[1:-1], scratch[-1]
    blocks = full_all[0].shape[0] // part
    count = len(near) + n_full + n_thin
    step = count * part + rank_part
    for some in made[:-1]:
        wait_all(some)
    for a in range(blocks):
        pieces = [full_all[0][(a ^ s) * part : ((a ^ s) + 1) * part, :] for s in near]
        pieces += [f[a * part : (a + 1) * part, :] for f in full_all[1:]]
        for j in range(n_thin):
            at = first + (j * blocks + a) * part
            pieces.append(act_all[at : at + part, :])
        pieces.append(act_all[act_all.shape[0] - rank_part :, :])
        lhs_all[a * step : (a + 1) * step, :] = jnp.concatenate(pieces, axis=0)
    wait_all(made[-1])
    for a in range(blocks):
        for r in range(ratio):
            h = a * ratio + r
            out = nn(lhs_all[a * step : (a + 1) * step, :], pre_all[:, h * blk : (h + 1) * blk])
            out = (out * scale).astype(BF16)
            for j in range(count):
                gu[h, j] = out[j * part : (j + 1) * part]
            gur[:, h * blk : (h + 1) * blk] = out[count * part :]


def up_pass(pres, acts, n_thin, full, near, part, rank_part, scale, blk):
    dp = len(pres)
    rows, hid = pres[0].shape
    count = len(near) + len(full) - 1 + n_thin
    args = [*pres, *acts, *full]
    blocks = full[0].shape[0] // part
    dims = [((acts[0].shape[0], dp * rows), BF16)] + [(f.shape, BF16) for f in full]
    dims += [((dp * rows, hid), BF16), ((blocks * (count * part + rank_part), dp * rows), BF16)]
    first = hid // blk * part
    return pl.pallas_call(
        functools.partial(
            up_kernel, near, len(full) - 1, n_thin, first, dp, hid // (blocks * blk), blk, rank_part, scale
        ),
        in_specs=[HBM] * len(args),
        out_specs=[VM, VM],
        out_shape=[shape((hid // blk, count, part, blk)), shape((rank_part, hid))],
        scratch_shapes=stacked(dims, len(args)),
        compiler_params=params(20),
        name="ku",
    )(*args)


def shards(tokens, cotangent, up_blocks, down_blocks, up_left, up_right, down_left, down_right):
    rows, width = tokens.shape
    blk = up_blocks.shape[-1]
    blocks = width // blk
    dp = lax.axis_size("dp")
    part, rank_part = blk // dp, up_left.shape[1] // dp
    scale = 1.0 / math.sqrt(rows * dp)
    near = tuple(s for s in STRIDES if s < blocks)
    masks = [s // blocks for s in STRIDES if s >= blocks]
    bits = [1 << b for b in range(dp.bit_length() - 1)]
    flip = bits[::-1]
    thin = [i for i, m in enumerate(masks) if m != 1]
    n = len(masks)
    tokens, cotangent, up_blocks, down_blocks = (in_hbm(x) for x in (tokens, cotangent, up_blocks, down_blocks))
    up_left, up_right, down_left, down_right = (in_hbm(x) for x in (up_left, up_right, down_left, down_right))

    tok_far = [swapped(tokens, "tensor", m) for m in masks]
    cot_far = [swapped(cotangent, "tensor", m) for m in masks]
    *lat_parts, both = latent_pass(tokens, cotangent, up_left, down_right)
    both = spread(both, bits)[1:]
    lat = total(*lat_parts)
    others = join_pass(both)
    far = [
        (cot_far[i], swapped(others, "tensor", m)) if m <= 2 else spread(cot_far[i], bits)
        for i, m in enumerate(masks)
    ]

    weights = (up_blocks, down_blocks, up_right, down_left)
    made = layer_half(dp, tuple(thin), tokens, tok_far, lat, *weights, near)
    acts, slope, out_here, out_parts, lat_down = made[:dp], made[dp], made[dp + 1], made[dp + 2 : -1], made[-1]
    made = layer_half(dp, (), cotangent, cot_far, lat, *weights, near, slope, lat_down)
    pre, grad_here, *grad_parts, lat_mine, lat_other = made
    out_parts = [swapped(x, "tensor", m) for x, m in zip(out_parts, masks)]
    grad_parts = [swapped(x, "tensor", m) for x, m in zip(grad_parts, masks)]
    act_groups = [x.reshape(-1, rows) for x in exchange(acts)]
    pre_groups = spread(pre, flip)
    *pieces, lat2 = cut_pass(total(lat_mine, lat_other), dp, rank_part)
    lat2_groups = exchange(pieces)

    hidden = up_blocks.shape[0]
    gd, own_rows, gul, gdr, *pieces = down_pass(
        tokens, cotangent, both, far, act_groups, lat2_groups, hidden, near, part, scale, blk
    )
    gdl, layer_out, token_grads = rank_pass(
        exchange(pieces), [out_here, grad_here, down_right, up_left, lat2, *out_parts, *grad_parts], n, blk
    )
    full_rows = [own_rows] + [swapped(own_rows, "tensor", m) for m in masks if m == 1]
    gu, gur = up_pass(pre_groups, act_groups, len(thin), full_rows, near, part, rank_part, scale, blk)
    return layer_out, token_grads, gu, gd, gul.T, gur, gdl.T, gdr


def solution(mesh):
    d, t = "dp", "tensor"
    blocks = P(t, None, None, None)
    in_specs = (P(d, t), P(d, t), blocks, blocks, P(t, None), P(None, t), P(t, None), P(None, t))
    cut = P(t, None, d, None)
    out_specs = (P(d, t), P(d, t), cut, cut, P(t, d), P(d, t), P(t, d), P(d, t))
    return jax.shard_map(shards, mesh=mesh, in_specs=in_specs, out_specs=out_specs, check_vma=False)
```

```python
import functools
import math

import jax
import jax.numpy as jnp
from jax import lax
from jax.experimental import pallas as pl
from jax.experimental.pallas import tpu as pltpu
from jax.sharding import PartitionSpec as P


STRIDES = (0, 1, 2, 4, 8, 16)
ROOT = math.sqrt(2.0 / math.pi)
CUBIC = 0.044715
F32 = jnp.float32
BF16 = jnp.bfloat16


def swapped(x, axis, mask):
    return lax.ppermute(x, axis, [(i, i ^ mask) for i in range(lax.axis_size(axis))])


def spread(x, order):
    got = {0: x}
    for mask in order:
        for m in list(got):
            got[m ^ mask] = swapped(got[m], "dp", mask)
    return [got[m] for m in range(len(got))]


def exchange(pieces):
    return [swapped(x, "dp", m) if m else x for m, x in enumerate(pieces)]


def total(mine, other):
    def add(x, y):
        return (x.astype(F32) + y.astype(F32)).astype(BF16)

    x = add(mine, swapped(other, "tensor", 1))
    mask = lax.axis_size("tensor") // 2
    while mask > 1:
        x = add(x, swapped(x, "tensor", mask))
        mask //= 2
    return x, swapped(x, "tensor", 1)


def nn(a, b):
    return jnp.dot(a, b, preferred_element_type=F32)


def nt(a, b):
    return lax.dot_general(a, b, (((1,), (1,)), ((), ())), preferred_element_type=F32)


def cols(block, blk):
    return pl.ds(pl.multiple_of(block * blk, blk), blk)


def one_hot(rows, width, first):
    r = lax.broadcasted_iota(jnp.int32, (rows, width), 0)
    c = lax.broadcasted_iota(jnp.int32, (rows, width), 1)
    return jnp.where(c == r + first, 1.0, 0.0).astype(BF16)


def params(mib=8):
    return pltpu.CompilerParams(vmem_limit_bytes=mib * 2**20)


VM = pl.BlockSpec(memory_space=pltpu.VMEM)
HBM = pl.BlockSpec(memory_space=pl.ANY)


def halves():
    c = lax.axis_index("tensor") & 1
    return c, 1 - c


def put_halves(dst, mine, other):
    n = mine.shape[0]
    for c, ref in zip(halves(), (mine, other)):
        dst[pl.ds(pl.multiple_of(c * n, n), n), :] = ref[...]


def get_halves(src, mine, other):
    n = mine.shape[0]
    for c, ref in zip(halves(), (mine, other)):
        ref[...] = src[pl.ds(pl.multiple_of(c * n, n), n), :]


def in_hbm(x):
    return pltpu.with_memory_space_constraint(x, pltpu.HBM)


def shape(dims, dtype=BF16):
    return jax.ShapeDtypeStruct(dims, dtype)


def wait_all(some):
    for c in some:
        c.wait()


class Copies:
    def __init__(self, sem):
        self.sem, self.count, self.out = sem, 0, []

    def start(self, src, dst):
        copy = pltpu.make_async_copy(src, dst, self.sem.at[self.count])
        self.count += 1
        copy.start()
        return copy

    def back(self, src, dst):
        self.out.append(self.start(src, dst))

    def finish(self):
        for copy in self.out:
            copy.wait()


def latent_kernel(tok, cot, ul, dr, mine, other, both, tmp, sem):
    rows = tok.shape[0]
    copies = Copies(sem)
    copies.back(tok, both.at[pl.ds(0, rows), :])
    copies.back(cot, both.at[pl.ds(rows, rows), :])
    tmp[:, :rows] = nn(tok[...], ul[...]).T.astype(BF16)
    tmp[:, rows:] = nt(dr[...], cot[...]).astype(BF16)
    get_halves(tmp, mine, other)
    copies.finish()


def latent_pass(tok, cot, ul, dr):
    rank, (rows, width) = dr.shape[0], tok.shape
    half = shape((rank // 2, 2 * rows))
    return pl.pallas_call(
        latent_kernel,
        in_specs=[VM] * 4,
        out_specs=[VM, VM, HBM],
        out_shape=[half, half, shape((2 * rows, width))],
        scratch_shapes=[pltpu.VMEM((rank, 2 * rows), BF16), pltpu.SemaphoreType.DMA((2,))],
        compiler_params=params(),
        name="kl",
    )(tok, cot, ul, dr)


def join_kernel(*refs):
    both, out, tmp, sem = refs[:-3], refs[-3], refs[-2], refs[-1]
    rows = both[0].shape[0] // 2
    copies = Copies(sem)
    spans = [pl.ds(g * rows, rows) for g in range(len(both))]
    reads = [copies.start(ref.at[pl.ds(rows, rows), :], tmp.at[g, :]) for ref, g in zip(both, spans)]
    for read, g in zip(reads, spans):
        read.wait()
        copies.back(tmp.at[g, :], out.at[g, :])
    copies.finish()


def join_pass(both):
    rows, width = both[0].shape[0] // 2, both[0].shape[1]
    dims = (len(both) * rows, width)
    return pl.pallas_call(
        join_kernel,
        in_specs=[HBM] * len(both),
        out_specs=HBM,
        out_shape=shape(dims),
        scratch_shapes=[pltpu.VMEM(dims, BF16), pltpu.SemaphoreType.DMA((2 * len(both),))],
        compiler_params=params(),
        name="kj",
    )(*both)


def half_kernel(back, near, thin, n, dp, ratio, blk, *refs):
    take = iter(refs)
    x_in = [next(take) for _ in range(1 + n)]
    lat_mine, lat_other, up, down, ur, dl = (next(take) for _ in range(6))
    slope_in, lat_down = (next(take), next(take)) if back else (None, None)
    act_outs = [next(take) for _ in range(1 if back else dp)]
    slope_out = None if back else next(take)
    here_out = next(take)
    parts_out = [next(take) for _ in range(n)]
    lat_outs = [next(take) for _ in range(2 if back else 1)]
    xs = [next(take) for _ in range(1 + n)]
    lat, up_v, down_v, ur_v, dl_v, slope = (next(take) for _ in range(6))
    act, here = next(take), next(take)
    parts = [next(take) for _ in range(n)]
    lat_tmp = next(take)
    lat_slabs = None if back else next(take)
    sem = next(take)
    rows, width = x_in[0].shape
    blocks = width // blk
    half = lat_mine.shape[0]
    copies = Copies(sem)

    def lat_half(src, c):
        return copies.start(src, lat.at[pl.ds(pl.multiple_of(c * half, half), half), :])

    first = [lat_half(src, c) for src, c in zip((lat_mine, lat_other), halves())]
    first += [copies.start(src, dst) for src, dst in zip(x_in, xs)]
    one, two = ((down, down_v), (up, up_v)) if back else ((up, up_v), (down, down_v))
    ones, twos = [], []
    if not back:
        first.append(copies.start(ur, ur_v))
    for a in range(blocks):
        span = pl.ds(a * ratio, ratio)
        now = []
        if back:
            piece = pl.ds(a * ratio * blk, ratio * blk)
            now = [copies.start(dl.at[piece, :], dl_v.at[piece, :]), copies.start(slope_in.at[a], slope.at[a])]
        ones.append(now + [copies.start(one[0].at[span], one[1].at[span])])
        rest = []
        if a == 0:
            rest.append(copies.start(ur, ur_v) if back else copies.start(dl, dl_v))
        twos.append(rest + [copies.start(two[0].at[span], two[1].at[span])])
    late = [copies.start(lat_down, lat_tmp)] if back else []
    part = blk // dp
    hidden = blocks * ratio
    for copy in first:
        copy.wait()
    if not back:
        for q in range(2 * dp):
            side, m = divmod(q, dp)
            lat_slabs[q] = lat[m * part : (m + 1) * part, side * rows : (side + 1) * rows]
        for z, i in enumerate(thin):
            for b in range(blocks):
                act[hidden + z * blocks + b] = xs[1 + i][:, b * blk : (b + 1) * blk].T
    lat_t = (lat[:, rows:] if back else lat[:, :rows]).T
    acc = jnp.zeros((rows, dl.shape[1]), F32)
    here[...] = jnp.zeros_like(here)
    for a in range(blocks):
        own = slice(a * blk, (a + 1) * blk)
        at = [slice((a ^ s) * blk, ((a ^ s) + 1) * blk) for s in near]
        pieces = [xs[0][:, c] for c in at] + [x[:, own] for x in xs[1:]]
        wait_all(ones[a])
        ys = []
        for r in range(ratio):
            h = a * ratio + r
            sl = slice(h * blk, (h + 1) * blk)
            if back:
                g = nt(lat_t, dl_v[sl, :])
                for j, piece in enumerate(pieces):
                    g = g + nt(piece, down_v[h, j])
                y = (g * slope[a, :, r * blk : (r + 1) * blk].astype(F32)).astype(BF16)
            else:
                v = nn(lat_t, ur_v[:, sl]) + nn(jnp.concatenate(pieces, axis=1), up_v[h].reshape(-1, blk))
                th = jnp.tanh(ROOT * (v + CUBIC * v * v * v))
                y = (0.5 * v * (1.0 + th)).astype(BF16)
                slope[a, :, r * blk : (r + 1) * blk] = (
                    0.5 * (1.0 + th)
                    + 0.5 * v * (1.0 - th * th) * ROOT * (1.0 + 3.0 * CUBIC * v * v)
                ).astype(BF16)
            if back:
                act[:, sl] = y
            else:
                act[h] = y.T
            ys.append(y)
        wait_all(twos[a])
        for r in range(ratio):
            h = a * ratio + r
            sl = slice(h * blk, (h + 1) * blk)
            acc = acc + (nt(ys[r], ur_v[:, sl]) if back else nn(ys[r], dl_v[sl, :]))
        if a == blocks - 1:
            if back:
                copies.back(act, act_outs[0])
            else:
                k, top = lax.axis_index("dp"), act.shape[0]
                for m, dst in enumerate(act_outs):
                    to = jnp.bitwise_xor(k, m)
                    copies.back(act.at[:, cols(to, part), :], dst.at[pl.ds(0, top)])
                    copies.back(lat_slabs.at[pl.ds(dp, dp)], dst.at[pl.ds(top, dp)])
                    copies.back(lat_slabs.at[to], dst.at[top + dp])
                copies.back(slope, slope_out)
        for j in list(range(len(near), len(near) + n)) + list(range(len(near))):
            f = sum(
                nt(ys[r], up_v[a * ratio + r, j]) if back else nn(ys[r], down_v[a * ratio + r, j])
                for r in range(ratio)
            )
            if j < len(near):
                here[:, at[j]] += f
            else:
                parts[j - len(near)][:, own] = f.astype(BF16)
        if a == blocks - 1:
            for src, dst in zip(parts, parts_out):
                copies.back(src, dst)
    copies.back(here, here_out)
    wait_all(late)
    if back:
        lat[:, :rows] = lat_tmp[...]
        lat[:, rows:] = acc.T.astype(BF16)
        for dst, c in zip(lat_outs, halves()):
            copies.back(lat.at[pl.ds(pl.multiple_of(c * half, half), half), :], dst)
    else:
        lat_tmp[...] = acc.T.astype(BF16)
        copies.back(lat_tmp, lat_outs[0])
    copies.finish()


def layer_half(dp, thin, x, far, lat, up, down, ur, dl, near, slope=None, lat_down=None):
    back = slope is not None
    rows, width = x.shape
    hidden, _, blk = up.shape[:3]
    blocks = width // blk
    ratio = hidden // blocks
    rank = dl.shape[1]
    n = len(far)
    block, gate, sums = shape((rows, width)), shape((blocks, rows, ratio * blk)), shape((rows, width), F32)
    tall, part = hidden + len(thin) * blocks, blk // dp
    wide = [shape((rows, hidden * blk))] if back else [shape((tall + dp + 1, part, rows))] * dp
    outs = wide + ([] if back else [gate]) + [sums] + [block] * n
    outs += [shape((rank // 2, 2 * rows))] * 2 if back else [shape((rank, rows))]
    held = [block] * (1 + n) + [shape((rank, 2 * rows))] + [shape(w.shape) for w in (up, down, ur, dl)]
    held += [gate, wide[0] if back else shape((tall, blk, rows)), sums] + [block] * n + [shape((rank, rows))] + ([] if back else [shape((2 * dp, part, rows))])
    args = [x, *far, *lat, up, down, ur, dl, *((slope, lat_down) if back else ())]
    return pl.pallas_call(
        functools.partial(half_kernel, back, near, thin, n, dp, ratio, blk),
        in_specs=[HBM] * len(args),
        out_specs=[HBM] * len(outs),
        out_shape=outs,
        scratch_shapes=[pltpu.VMEM(h.shape, h.dtype) for h in held]
        + [pltpu.SemaphoreType.DMA((len(args) + len(outs) + 4 * blocks + 2 * dp,))],
        compiler_params=params(28),
    )(*args)


def gather_copies(groups, scratch, sem):
    copies = Copies(sem)
    made = []
    for refs, dst in zip(groups, scratch):
        rows, width = refs[0].shape
        side = dst.shape[0] == rows
        made.append(
            [
                copies.start(
                    ref, dst.at[:, pl.ds(m * width, width)] if side else dst.at[pl.ds(m * rows, rows), :]
                )
                for m, ref in enumerate(refs)
            ]
        )
    return made


def split_groups(first, both, base):
    rows = first.shape[0]
    return [first] + [ref.at[pl.ds(base * rows, rows), :] for ref in both]


def down_kernel(near, kinds, dp, ratio, blk, rank_part, scale, *refs):
    take = iter(refs)
    tok, cot = next(take), next(take)
    both = [next(take) for _ in range(dp - 1)]
    rows, width = tok.shape
    cots = [split_groups(cot, both, 1)]
    for joint in kinds:
        if joint:
            far, rest = next(take), next(take)
            cots.append([far] + [rest.at[pl.ds(g * rows, rows), :] for g in range(dp - 1)])
        else:
            cots.append([next(take) for _ in range(dp)])
    acts = [next(take) for _ in range(dp)]
    lats = [next(take) for _ in range(dp)]
    gd, own_rows, gul, gdr = (next(take) for _ in range(4))
    lats = [ref.at[:, pl.ds(0, 2 * rows)] for ref in lats]
    tok_all = next(take)
    cot_all = [next(take) for _ in cots]
    act_all, lat_all = next(take), next(take)
    made = gather_copies(
        [split_groups(tok, both, 0), acts] + cots + [lats], [tok_all, act_all] + cot_all + [lat_all], next(take)
    )
    blocks = width // blk
    part = gd.shape[2]
    k = lax.axis_index("dp")
    pick = one_hot(part, blk, k * part)
    wait_all(made[0])
    for b in range(blocks):
        own_rows[b * part : (b + 1) * part, :] = nt(pick, tok_all[:, b * blk : (b + 1) * blk]).astype(BF16)
    for some in made[1:]:
        wait_all(some)

    def lat_rows(half):
        return jnp.concatenate(
            [
                lat_all[m * rank_part : (m + 1) * rank_part, half * rows : (half + 1) * rows]
                for m in range(dp)
            ],
            axis=1,
        )

    gdr[...] = (nn(lat_rows(0), cot_all[0][...]) * scale).astype(BF16)
    gul[...] = (nn(lat_rows(1), tok_all[...]) * scale).astype(BF16)
    for a in range(blocks):
        lhs = act_all[a * ratio * part : (a + 1) * ratio * part, :]
        srcs = [(0, a ^ s) for s in near] + [(1 + j, a) for j in range(len(kinds))]
        for j, (i, b) in enumerate(srcs):
            out = (nn(lhs, cot_all[i][:, b * blk : (b + 1) * blk]) * scale).astype(BF16)
            for r in range(ratio):
                gd[a * ratio + r, j] = out[r * part : (r + 1) * part]


def stacked(dims, count):
    return [pltpu.VMEM(d, t) for d, t in dims] + [pltpu.SemaphoreType.DMA((count,))]


def cut_kernel(dp, count, scale, *refs):
    mine, other, acts, outs, whole = refs[0], refs[1], refs[2 : 2 + dp], refs[2 + dp : 2 + 2 * dp], refs[2 + 2 * dp]
    act_all, out_all, sem = refs[3 + 2 * dp :]
    rank_part, width = outs[0].shape
    made = gather_copies([acts], [act_all], sem)
    put_halves(whole, mine, other)
    wait_all(made[0])
    tall = act_all.shape[0]
    lat_cot = act_all[tall - (dp + 1) * rank_part : tall - rank_part, :]
    out_all[...] = (nt(lat_cot, act_all[:count, :]) * scale).astype(BF16)
    for m in range(dp):
        rows = cols(jnp.bitwise_xor(lax.axis_index("dp"), m), rank_part)
        outs[m][:, : width - count] = whole[rows, :]
        outs[m][:, width - count :] = out_all[rows, :]


def cut_pass(lat, acts, count, rank_part, scale):
    dp, rank = len(acts), 2 * lat[0].shape[0]
    tall, rows = acts[0].shape
    piece = shape((rank_part, 2 * rows + count))
    return pl.pallas_call(
        functools.partial(cut_kernel, dp, count, scale),
        in_specs=[VM] * 2 + [HBM] * dp,
        out_specs=[VM] * (dp + 1),
        out_shape=[piece] * dp + [shape((rank, 2 * rows))],
        scratch_shapes=stacked([((tall, dp * rows), BF16), ((rank, count), BF16)], dp),
        compiler_params=params(),
        name="kc",
    )(*lat, *acts)


def down_pass(tok, cot, both, far, acts, lats, hidden, near, part, scale, blk):
    dp = len(acts)
    rows, width = tok.shape
    rank_part = lats[0].shape[0]
    kinds = tuple(len(f) == 2 for f in far)
    args = [tok, cot, *both, *[x for f in far for x in f], *acts, *lats]
    dims = [((dp * rows, width), BF16), ((acts[0].shape[0], dp * rows), BF16)]
    dims = dims[:1] + [((dp * rows, width), BF16)] * (1 + len(far)) + dims[1:]
    dims += [((dp * rank_part, 2 * rows), BF16)]
    wide = shape((rank_part, width))
    return pl.pallas_call(
        functools.partial(down_kernel, near, kinds, dp, hidden * blk // width, blk, rank_part, scale),
        in_specs=[HBM] * len(args),
        out_specs=[VM] * 4,
        out_shape=[
            shape((hidden, len(near) + len(far), part, blk)),
            shape((width // blk * part, dp * rows)),
            wide,
            wide,
        ],
        scratch_shapes=stacked(dims, dp * len(dims)),
        compiler_params=params(24),
        name="kd",
    )(*args)


def rank_kernel(n, dp, blk, *refs):
    take = iter(refs)
    pieces = [next(take) for _ in range(dp)]
    singles = [[next(take)] for _ in range(5 + 2 * n)]
    gdl, layer_out, token_grads = (next(take) for _ in range(3))
    count = gdl.shape[1] // dp
    groups = [[ref.at[:, pl.ds(ref.shape[1] - count, count)] for ref in pieces]] + singles
    scratch = [next(take) for _ in groups]
    made = gather_copies(groups, scratch, next(take))
    gdl_all, out_here, grad_here, dr, ul, lat2 = scratch[:6]
    rows = out_here.shape[0]
    part = blk // dp
    rank_part = pieces[0].shape[0]
    some = min(count, max(128, part))
    each = some // part * blk
    r = lax.broadcasted_iota(jnp.int32, (some, each), 0)
    c = lax.broadcasted_iota(jnp.int32, (some, each), 1)
    places = [
        jnp.where(
            c == r // part * blk + jnp.bitwise_xor(lax.axis_index("dp"), m) * part + r % part, 1.0, 0.0
        ).astype(BF16)
        for m in range(dp)
    ]
    wait_all(made[0])
    for g in range(count // some):
        out = sum(
            nn(gdl_all[m * rank_part : (m + 1) * rank_part, g * some : (g + 1) * some], places[m])
            for m in range(dp)
        )
        gdl[:, g * each : (g + 1) * each] = out.astype(BF16)
    for some in made[1:]:
        wait_all(some)
    out = out_here[...] + nn(lat2[:, :rows].T, dr[...])
    grad = grad_here[...] + nt(lat2[:, rows:].T, ul[...])
    for p, q in zip(scratch[6 : 6 + n], scratch[6 + n :]):
        out = out + p[...].astype(F32)
        grad = grad + q[...].astype(F32)
    layer_out[...] = out.astype(BF16)
    token_grads[...] = grad.astype(BF16)


def rank_pass(pieces, singles, n, count, blk):
    dp, rank_part = len(pieces), pieces[0].shape[0]
    args = [*pieces, *singles]
    dims = [((dp * rank_part, count), BF16)] + [(x.shape, x.dtype) for x in singles]
    full = shape(singles[0].shape)
    return pl.pallas_call(
        functools.partial(rank_kernel, n, dp, blk),
        in_specs=[HBM] * len(args),
        out_specs=[VM] * 3,
        out_shape=[shape((rank_part, count * dp)), full, full],
        scratch_shapes=stacked(dims, len(args)),
        compiler_params=params(16),
        name="kr",
    )(*args)


def up_kernel(near, n_full, n_thin, first, dp, ratio, blk, rank_part, scale, *refs):
    take = iter(refs)
    pres, acts = ([next(take) for _ in range(dp)] for _ in range(2))
    full = [[next(take)] for _ in range(1 + n_full)]
    gu, gur = next(take), next(take)
    groups = [acts] + full + [pres]
    scratch = [next(take) for _ in groups]
    lhs_all, sem = next(take), next(take)
    made = gather_copies(groups, scratch, sem)
    part = gu.shape[2]
    act_all, full_all, pre_all = scratch[0], scratch[1:-1], scratch[-1]
    blocks = full_all[0].shape[0] // part
    count = len(near) + n_full + n_thin
    step = count * part + rank_part
    for some in made[:-1]:
        wait_all(some)
    for a in range(blocks):
        pieces = [full_all[0][(a ^ s) * part : ((a ^ s) + 1) * part, :] for s in near]
        pieces += [f[a * part : (a + 1) * part, :] for f in full_all[1:]]
        for j in range(n_thin):
            at = first + (j * blocks + a) * part
            pieces.append(act_all[at : at + part, :])
        pieces.append(act_all[act_all.shape[0] - rank_part :, :])
        lhs_all[a * step : (a + 1) * step, :] = jnp.concatenate(pieces, axis=0)
    wait_all(made[-1])
    for a in range(blocks):
        for r in range(ratio):
            h = a * ratio + r
            out = nn(lhs_all[a * step : (a + 1) * step, :], pre_all[:, h * blk : (h + 1) * blk])
            out = (out * scale).astype(BF16)
            for j in range(count):
                gu[h, j] = out[j * part : (j + 1) * part]
            gur[:, h * blk : (h + 1) * blk] = out[count * part :]


def up_pass(pres, acts, n_thin, full, near, part, rank_part, scale, blk):
    dp = len(pres)
    rows, hid = pres[0].shape
    count = len(near) + len(full) - 1 + n_thin
    args = [*pres, *acts, *full]
    blocks = full[0].shape[0] // part
    dims = [((acts[0].shape[0], dp * rows), BF16)] + [(f.shape, BF16) for f in full]
    dims += [((dp * rows, hid), BF16), ((blocks * (count * part + rank_part), dp * rows), BF16)]
    first = hid // blk * part
    return pl.pallas_call(
        functools.partial(
            up_kernel, near, len(full) - 1, n_thin, first, dp, hid // (blocks * blk), blk, rank_part, scale
        ),
        in_specs=[HBM] * len(args),
        out_specs=[VM, VM],
        out_shape=[shape((hid // blk, count, part, blk)), shape((rank_part, hid))],
        scratch_shapes=stacked(dims, len(args)),
        compiler_params=params(20),
        name="ku",
    )(*args)


def shards(tokens, cotangent, up_blocks, down_blocks, up_left, up_right, down_left, down_right):
    rows, width = tokens.shape
    blk = up_blocks.shape[-1]
    blocks = width // blk
    dp = lax.axis_size("dp")
    part, rank_part = blk // dp, up_left.shape[1] // dp
    scale = 1.0 / math.sqrt(rows * dp)
    near = tuple(s for s in STRIDES if s < blocks)
    masks = [s // blocks for s in STRIDES if s >= blocks]
    bits = [1 << b for b in range(dp.bit_length() - 1)]
    flip = bits[::-1]
    thin = [i for i, m in enumerate(masks) if m != 1]
    n = len(masks)
    tokens, cotangent, up_blocks, down_blocks = (in_hbm(x) for x in (tokens, cotangent, up_blocks, down_blocks))
    up_left, up_right, down_left, down_right = (in_hbm(x) for x in (up_left, up_right, down_left, down_right))

    tok_far = [swapped(tokens, "tensor", m) for m in masks]
    cot_far = [swapped(cotangent, "tensor", m) for m in masks]
    *lat_parts, both = latent_pass(tokens, cotangent, up_left, down_right)
    both = spread(both, bits)[1:]
    lat = total(*lat_parts)
    others = join_pass(both)
    far = [
        (cot_far[i], swapped(others, "tensor", m)) if m <= 2 else spread(cot_far[i], bits)
        for i, m in enumerate(masks)
    ]

    weights = (up_blocks, down_blocks, up_right, down_left)
    made = layer_half(dp, tuple(thin), tokens, tok_far, lat, *weights, near)
    acts, slope, out_here, out_parts, lat_down = made[:dp], made[dp], made[dp + 1], made[dp + 2 : -1], made[-1]
    made = layer_half(dp, (), cotangent, cot_far, lat, *weights, near, slope, lat_down)
    pre, grad_here, *grad_parts, lat_mine, lat_other = made
    out_parts = [swapped(x, "tensor", m) for x, m in zip(out_parts, masks)]
    grad_parts = [swapped(x, "tensor", m) for x, m in zip(grad_parts, masks)]
    act_groups = [x.reshape(-1, rows) for x in exchange(acts)]
    pre_groups = spread(pre, flip)
    hidden = up_blocks.shape[0]
    *pieces, lat2 = cut_pass(total(lat_mine, lat_other), act_groups, hidden * part, rank_part, scale)
    pieces = exchange(pieces)
    gd, own_rows, gul, gdr = down_pass(
        tokens, cotangent, both, far, act_groups, pieces, hidden, near, part, scale, blk
    )
    gdl, layer_out, token_grads = rank_pass(
        pieces, [out_here, grad_here, down_right, up_left, lat2, *out_parts, *grad_parts], n, hidden * part, blk
    )
    full_rows = [own_rows] + [swapped(own_rows, "tensor", m) for m in masks if m == 1]
    gu, gur = up_pass(pre_groups, act_groups, len(thin), full_rows, near, part, rank_part, scale, blk)
    return layer_out, token_grads, gu, gd, gul.T, gur, gdl.T, gdr


def solution(mesh):
    d, t = "dp", "tensor"
    blocks = P(t, None, None, None)
    in_specs = (P(d, t), P(d, t), blocks, blocks, P(t, None), P(None, t), P(t, None), P(None, t))
    cut = P(t, None, d, None)
    out_specs = (P(d, t), P(d, t), cut, cut, P(t, d), P(d, t), P(t, d), P(d, t))
    return jax.shard_map(shards, mesh=mesh, in_specs=in_specs, out_specs=out_specs, check_vma=False)
```

```python
import functools
import math

import jax
import jax.numpy as jnp
from jax import lax
from jax.experimental import pallas as pl
from jax.experimental.pallas import tpu as pltpu
from jax.sharding import PartitionSpec as P


STRIDES = (0, 1, 2, 4, 8, 16)
ROOT = math.sqrt(2.0 / math.pi)
CUBIC = 0.044715
F32 = jnp.float32
BF16 = jnp.bfloat16


def swapped(x, axis, mask):
    return lax.ppermute(x, axis, [(i, i ^ mask) for i in range(lax.axis_size(axis))])


def spread(x, order):
    got = {0: x}
    for mask in order:
        for m in list(got):
            got[m ^ mask] = swapped(got[m], "dp", mask)
    return [got[m] for m in range(len(got))]


def exchange(pieces):
    return [swapped(x, "dp", m) if m else x for m, x in enumerate(pieces)]


def total(mine, other):
    def add(x, y):
        return (x.astype(F32) + y.astype(F32)).astype(BF16)

    x = add(mine, swapped(other, "tensor", 1))
    mask = lax.axis_size("tensor") // 2
    while mask > 1:
        x = add(x, swapped(x, "tensor", mask))
        mask //= 2
    return x, swapped(x, "tensor", 1)


def nn(a, b):
    return jnp.dot(a, b, preferred_element_type=F32)


def nt(a, b):
    return lax.dot_general(a, b, (((1,), (1,)), ((), ())), preferred_element_type=F32)


def cols(block, blk):
    return pl.ds(pl.multiple_of(block * blk, blk), blk)


def one_hot(rows, width, first):
    r = lax.broadcasted_iota(jnp.int32, (rows, width), 0)
    c = lax.broadcasted_iota(jnp.int32, (rows, width), 1)
    return jnp.where(c == r + first, 1.0, 0.0).astype(BF16)


def params(mib=8, **more):
    return pltpu.CompilerParams(vmem_limit_bytes=mib * 2**20, **more)


VM = pl.BlockSpec(memory_space=pltpu.VMEM)
HBM = pl.BlockSpec(memory_space=pl.ANY)


def halves():
    c = lax.axis_index("tensor") & 1
    return c, 1 - c


def put_halves(dst, mine, other):
    n = mine.shape[0]
    for c, ref in zip(halves(), (mine, other)):
        dst[pl.ds(pl.multiple_of(c * n, n), n), :] = ref[...]


def get_halves(src, mine, other):
    n = mine.shape[0]
    for c, ref in zip(halves(), (mine, other)):
        ref[...] = src[pl.ds(pl.multiple_of(c * n, n), n), :]


def in_hbm(x):
    return pltpu.with_memory_space_constraint(x, pltpu.HBM)


def shape(dims, dtype=BF16):
    return jax.ShapeDtypeStruct(dims, dtype)


def wait_all(some):
    for c in some:
        c.wait()


class Copies:
    def __init__(self, sem):
        self.sem, self.count, self.out = sem, 0, []

    def start(self, src, dst):
        copy = pltpu.make_async_copy(src, dst, self.sem.at[self.count])
        self.count += 1
        copy.start()
        return copy

    def back(self, src, dst):
        self.out.append(self.start(src, dst))

    def finish(self):
        for copy in self.out:
            copy.wait()


def latent_kernel(tok, cot, ul, dr, mine, other, both, tmp, sem):
    rows = tok.shape[0]
    copies = Copies(sem)
    copies.back(tok, both.at[pl.ds(0, rows), :])
    copies.back(cot, both.at[pl.ds(rows, rows), :])
    tmp[:, :rows] = nn(tok[...], ul[...]).T.astype(BF16)
    tmp[:, rows:] = nt(dr[...], cot[...]).astype(BF16)
    get_halves(tmp, mine, other)
    copies.finish()


def latent_pass(tok, cot, ul, dr):
    rank, (rows, width) = dr.shape[0], tok.shape
    half = shape((rank // 2, 2 * rows))
    return pl.pallas_call(
        latent_kernel,
        in_specs=[VM] * 4,
        out_specs=[VM, VM, HBM],
        out_shape=[half, half, shape((2 * rows, width))],
        scratch_shapes=[pltpu.VMEM((rank, 2 * rows), BF16), pltpu.SemaphoreType.DMA((2,))],
        compiler_params=params(),
        name="kl",
    )(tok, cot, ul, dr)


def rest_groups(dp):
    return [m for m in range(1, dp) if m != dp // 2], dp // 2


def join_kernel(*refs):
    both, out, alone, tmp, sem = refs[:-4], refs[-4], refs[-3], refs[-2], refs[-1]
    rows = both[0].shape[0] // 2
    copies = Copies(sem)
    spans = [pl.ds(g * rows, rows) for g in range(len(both))]
    reads = [copies.start(ref.at[pl.ds(rows, rows), :], tmp.at[g, :]) for ref, g in zip(both, spans)]
    rest, one = rest_groups(len(both) + 1)
    for read, g, m in zip(reads, spans, range(1, len(both) + 1)):
        read.wait()
        copies.back(tmp.at[g, :], alone if m == one else out.at[spans[rest.index(m)], :])
    copies.finish()


def join_pass(both):
    rows, width = both[0].shape[0] // 2, both[0].shape[1]
    n = len(both)
    return pl.pallas_call(
        join_kernel,
        in_specs=[HBM] * n,
        out_specs=[HBM] * 2,
        out_shape=[shape(((n - 1) * rows, width)), shape((rows, width))],
        scratch_shapes=[pltpu.VMEM((n * rows, width), BF16), pltpu.SemaphoreType.DMA((2 * n,))],
        compiler_params=params(),
        name="kj",
    )(*both)


def half_kernel(back, near, thin, n, dp, ratio, blk, *refs):
    take = iter(refs)
    x_in = [next(take) for _ in range(1 + n)]
    lat_mine, lat_other, up, down, ur, dl = (next(take) for _ in range(6))
    slope_in, lat_down = (next(take), next(take)) if back else (None, None)
    act_outs = [next(take) for _ in range(2 if back else dp)]
    slope_out = None if back else next(take)
    here_out = next(take)
    parts_out = [next(take) for _ in range(n)]
    lat_outs = [next(take) for _ in range(2 if back else 1)]
    xs = [next(take) for _ in range(1 + n)]
    lat, up_v, down_v, ur_v, dl_v, slope = (next(take) for _ in range(6))
    act, here = next(take), next(take)
    parts = [next(take) for _ in range(n)]
    lat_tmp = next(take)
    lat_slabs = None if back else next(take)
    sem = next(take)
    rows, width = x_in[0].shape
    blocks = width // blk
    half = lat_mine.shape[0]
    copies = Copies(sem)

    def lat_half(src, c):
        return copies.start(src, lat.at[pl.ds(pl.multiple_of(c * half, half), half), :])

    first = [lat_half(src, c) for src, c in zip((lat_mine, lat_other), halves())]
    first += [copies.start(src, dst) for src, dst in zip(x_in, xs)]
    one, two = ((down, down_v), (up, up_v)) if back else ((up, up_v), (down, down_v))
    ones, twos = [], []
    if not back:
        first.append(copies.start(ur, ur_v))
    for a in range(blocks):
        span = pl.ds(a * ratio, ratio)
        now = []
        if back:
            piece = pl.ds(a * ratio * blk, ratio * blk)
            now = [copies.start(dl.at[piece, :], dl_v.at[piece, :]), copies.start(slope_in.at[a], slope.at[a])]
        ones.append(now + [copies.start(one[0].at[span], one[1].at[span])])
        rest = []
        if a == 0:
            rest.append(copies.start(ur, ur_v) if back else copies.start(dl, dl_v))
        twos.append(rest + [copies.start(two[0].at[span], two[1].at[span])])
    late = [copies.start(lat_down, lat_tmp)] if back else []
    part = blk // dp
    hidden = blocks * ratio
    for copy in first:
        copy.wait()
    if not back:
        for q in range(2 * dp):
            side, m = divmod(q, dp)
            lat_slabs[q] = lat[m * part : (m + 1) * part, side * rows : (side + 1) * rows]
        for z, i in enumerate(thin):
            for b in range(blocks):
                act[hidden + z * blocks + b] = xs[1 + i][:, b * blk : (b + 1) * blk].T
    lat_t = (lat[:, rows:] if back else lat[:, :rows]).T
    acc = jnp.zeros((rows, dl.shape[1]), F32)
    here[...] = jnp.zeros_like(here)
    for a in range(blocks):
        own = slice(a * blk, (a + 1) * blk)
        at = [slice((a ^ s) * blk, ((a ^ s) + 1) * blk) for s in near]
        pieces = [xs[0][:, c] for c in at] + [x[:, own] for x in xs[1:]]
        wait_all(ones[a])
        ys = []
        for r in range(ratio):
            h = a * ratio + r
            sl = slice(h * blk, (h + 1) * blk)
            if back:
                g = nt(lat_t, dl_v[sl, :])
                for j, piece in enumerate(pieces):
                    g = g + nt(piece, down_v[h, j])
                y = (g * slope[a, :, r * blk : (r + 1) * blk].astype(F32)).astype(BF16)
            else:
                v = nn(lat_t, ur_v[:, sl]) + nn(jnp.concatenate(pieces, axis=1), up_v[h].reshape(-1, blk))
                th = jnp.tanh(ROOT * (v + CUBIC * v * v * v))
                y = (0.5 * v * (1.0 + th)).astype(BF16)
                slope[a, :, r * blk : (r + 1) * blk] = (
                    0.5 * (1.0 + th)
                    + 0.5 * v * (1.0 - th * th) * ROOT * (1.0 + 3.0 * CUBIC * v * v)
                ).astype(BF16)
            if back:
                act[:, sl] = y
            else:
                act[h] = y.T
            ys.append(y)
        wait_all(twos[a])
        for r in range(ratio):
            h = a * ratio + r
            sl = slice(h * blk, (h + 1) * blk)
            acc = acc + (nt(ys[r], ur_v[:, sl]) if back else nn(ys[r], dl_v[sl, :]))
        if a == blocks - 1:
            if back:
                for q, dst in enumerate(act_outs):
                    copies.back(act.at[:, pl.ds(q * dst.shape[1], dst.shape[1])], dst)
            else:
                k, top = lax.axis_index("dp"), act.shape[0]
                for m, dst in enumerate(act_outs):
                    to = jnp.bitwise_xor(k, m)
                    copies.back(act.at[:, cols(to, part), :], dst.at[pl.ds(0, top)])
                    copies.back(lat_slabs.at[pl.ds(dp, dp)], dst.at[pl.ds(top, dp)])
                    copies.back(lat_slabs.at[to], dst.at[top + dp])
                copies.back(slope, slope_out)
        for j in list(range(len(near), len(near) + n)) + list(range(len(near))):
            f = sum(
                nt(ys[r], up_v[a * ratio + r, j]) if back else nn(ys[r], down_v[a * ratio + r, j])
                for r in range(ratio)
            )
            if j < len(near):
                here[:, at[j]] += f
            else:
                parts[j - len(near)][:, own] = f.astype(BF16)
        if a == blocks - 1:
            for src, dst in zip(parts, parts_out):
                copies.back(src, dst)
    copies.back(here, here_out)
    wait_all(late)
    if back:
        lat[:, :rows] = lat_tmp[...]
        lat[:, rows:] = acc.T.astype(BF16)
        for dst, c in zip(lat_outs, halves()):
            copies.back(lat.at[pl.ds(pl.multiple_of(c * half, half), half), :], dst)
    else:
        lat_tmp[...] = acc.T.astype(BF16)
        copies.back(lat_tmp, lat_outs[0])
    copies.finish()


def layer_half(dp, thin, x, far, lat, up, down, ur, dl, near, slope=None, lat_down=None):
    back = slope is not None
    rows, width = x.shape
    hidden, _, blk = up.shape[:3]
    blocks = width // blk
    ratio = hidden // blocks
    rank = dl.shape[1]
    n = len(far)
    block, gate, sums = shape((rows, width)), shape((blocks, rows, ratio * blk)), shape((rows, width), F32)
    tall, part = hidden + len(thin) * blocks, blk // dp
    wide = [shape((rows, hidden * blk // 2))] * 2 if back else [shape((tall + dp + 1, part, rows))] * dp
    outs = wide + ([] if back else [gate]) + [sums] + [block] * n
    outs += [shape((rank // 2, 2 * rows))] * 2 if back else [shape((rank, rows))]
    held = [block] * (1 + n) + [shape((rank, 2 * rows))] + [shape(w.shape) for w in (up, down, ur, dl)]
    held += [gate, shape((rows, hidden * blk)) if back else shape((tall, blk, rows)), sums] + [block] * n + [shape((rank, rows))] + ([] if back else [shape((2 * dp, part, rows))])
    args = [x, *far, *lat, up, down, ur, dl, *((slope, lat_down) if back else ())]
    return pl.pallas_call(
        functools.partial(half_kernel, back, near, thin, n, dp, ratio, blk),
        in_specs=[HBM] * len(args),
        out_specs=[HBM] * len(outs),
        out_shape=outs,
        scratch_shapes=[pltpu.VMEM(h.shape, h.dtype) for h in held]
        + [pltpu.SemaphoreType.DMA((len(args) + len(outs) + 4 * blocks + 2 * dp,))],
        compiler_params=params(28),
    )(*args)


def gather_copies(groups, scratch, sem):
    copies = sem if isinstance(sem, Copies) else Copies(sem)
    made = []
    for refs, dst in zip(groups, scratch):
        rows, width = refs[0].shape
        side = dst.shape[0] == rows
        made.append(
            [
                copies.start(
                    ref, dst.at[:, pl.ds(m * width, width)] if side else dst.at[pl.ds(m * rows, rows), :]
                )
                for m, ref in enumerate(refs)
            ]
        )
    return made


def split_groups(first, both, base):
    rows = first.shape[0]
    return [first] + [ref.at[pl.ds(base * rows, rows), :] for ref in both]


def down_kernel(near, kinds, dp, ratio, blk, scale, *refs):
    take = iter(refs)
    cot = next(take)
    both = [next(take) for _ in range(dp - 1)]
    rows, width = cot.shape
    cots = [split_groups(cot, both, 1)]
    for joint in kinds:
        if joint:
            far, rest, alone = (next(take) for _ in range(3))
            order, one = rest_groups(dp)
            some = {0: far, one: alone}
            some.update({m: rest.at[pl.ds(g * rows, rows), :] for g, m in enumerate(order)})
            cots.append([some[m] for m in range(dp)])
        else:
            cots.append([next(take) for _ in range(dp)])
    acts = [next(take) for _ in range(dp)]
    gd = next(take)
    cot_all = [next(take) for _ in cots]
    act_all = next(take)
    made = gather_copies(cots + [acts], cot_all + [act_all], next(take))
    blocks = width // blk
    part = gd.shape[2]
    for some in made:
        wait_all(some)
    for a in range(blocks):
        lhs = act_all[a * ratio * part : (a + 1) * ratio * part, :]
        srcs = [(0, a ^ s) for s in near] + [(1 + j, a) for j in range(len(kinds))]
        for j, (i, b) in enumerate(srcs):
            out = (nn(lhs, cot_all[i][:, b * blk : (b + 1) * blk]) * scale).astype(BF16)
            for r in range(ratio):
                gd[a * ratio + r, j] = out[r * part : (r + 1) * part]


def stacked(dims, count):
    return [pltpu.VMEM(d, t) for d, t in dims] + [pltpu.SemaphoreType.DMA((count,))]


def cut_kernel(dp, count, part, scale, *refs):
    take = iter(refs)
    mine, other, tok = (next(take) for _ in range(3))
    both = [next(take) for _ in range(dp - 1)]
    acts, outs = ([next(take) for _ in range(dp)] for _ in range(2))
    whole, own_rows, act_all, tok_all, out_all, sem = (next(take) for _ in range(6))
    rank_part, width = outs[0].shape
    made = gather_copies([acts, split_groups(tok, both, 0)], [act_all, tok_all], sem)
    put_halves(whole, mine, other)
    wait_all(made[0])
    tall = act_all.shape[0]
    lat_cot = act_all[tall - (dp + 1) * rank_part : tall - rank_part, :]
    out_all[...] = (nt(lat_cot, act_all[:count, :]) * scale).astype(BF16)
    for m in range(dp):
        rows = cols(jnp.bitwise_xor(lax.axis_index("dp"), m), rank_part)
        outs[m][:, : width - count] = whole[rows, :]
        outs[m][:, width - count :] = out_all[rows, :]
    wait_all(made[1])
    blk = dp * part
    pick = one_hot(part, blk, lax.axis_index("dp") * part)
    for b in range(tok.shape[1] // blk):
        own_rows[b * part : (b + 1) * part, :] = nt(pick, tok_all[:, b * blk : (b + 1) * blk]).astype(BF16)


def cut_pass(lat, tok, both, acts, count, part, rank_part, scale):
    dp, rank = len(acts), 2 * lat[0].shape[0]
    tall, rows = acts[0].shape
    piece = shape((rank_part, 2 * rows + count))
    return pl.pallas_call(
        functools.partial(cut_kernel, dp, count, part, scale),
        in_specs=[VM] * 2 + [HBM] * (2 * dp),
        out_specs=[VM] * (dp + 2),
        out_shape=[piece] * dp + [shape((rank, 2 * rows)), shape((tok.shape[1] // dp, dp * rows))],
        scratch_shapes=stacked(
            [((tall, dp * rows), BF16), ((dp * rows, tok.shape[1]), BF16), ((rank, count), BF16)], 2 * dp
        ),
        compiler_params=params(),
        name="kc",
    )(*lat, tok, *both, *acts)


def down_pass(cot, both, far, acts, hidden, near, part, scale, blk):
    dp = len(acts)
    rows, width = cot.shape
    kinds = tuple(isinstance(f, tuple) for f in far)
    args = [cot, *both, *[x for f in far for x in f], *acts]
    dims = [((dp * rows, width), BF16)] * (1 + len(far)) + [((acts[0].shape[0], dp * rows), BF16)]
    return pl.pallas_call(
        functools.partial(down_kernel, near, kinds, dp, hidden * blk // width, blk, scale),
        in_specs=[HBM] * len(args),
        out_specs=VM,
        out_shape=shape((hidden, len(near) + len(far), part, blk)),
        scratch_shapes=stacked(dims, dp * len(dims)),
        compiler_params=params(24),
        name="kd",
    )(*args)


def finish_kernel(n, *refs):
    args, outs, scratch = refs[: 5 + 2 * n], refs[5 + 2 * n : 7 + 2 * n], refs[7 + 2 * n : -1]
    copies = Copies(refs[-1])
    made = [copies.start(src, dst) for src, dst in zip(args, scratch)]
    rows = outs[0].shape[0]
    lat2, down_right, up_left, here = scratch[0], scratch[1], scratch[2], scratch[3:5]
    wait_all(made[:5])
    sums = [
        here[0][...] + nn(lat2[:, :rows].T, down_right[...]),
        here[1][...] + nt(lat2[:, rows:].T, up_left[...]),
    ]
    for q, out in enumerate(outs):
        some = slice(5 + q * n, 5 + (q + 1) * n)
        wait_all(made[some])
        for p in scratch[some]:
            sums[q] = sums[q] + p[...].astype(F32)
        out[...] = sums[q].astype(BF16)


def finish_pass(lat2, down_right, up_left, out_here, grad_here, out_parts, grad_parts):
    args = [lat2, down_right, up_left, out_here, grad_here, *out_parts, *grad_parts]
    return pl.pallas_call(
        functools.partial(finish_kernel, len(out_parts)),
        in_specs=[HBM] * len(args),
        out_specs=[VM] * 2,
        out_shape=[shape(out_here.shape)] * 2,
        scratch_shapes=stacked([(x.shape, x.dtype) for x in args], len(args)),
        compiler_params=params(),
        name="kz",
    )(*args)


def rank_kernel(dp, blk, scale, *refs):
    take = iter(refs)
    tok, cot = next(take), next(take)
    both = [next(take) for _ in range(dp - 1)]
    pieces = [next(take) for _ in range(dp)]
    gdl, gul, gdr = (next(take) for _ in range(3))
    rows = tok.shape[0]
    rank_part, tall = pieces[0].shape
    groups = [split_groups(tok, both, 0), split_groups(cot, both, 1), pieces]
    scratch = [next(take) for _ in groups]
    made = gather_copies(groups, scratch, next(take))
    tok_all, cot_all, all_pieces = scratch
    part, count = blk // dp, tall - 2 * rows
    some = min(count, max(128, part))
    each = some // part * blk
    r = lax.broadcasted_iota(jnp.int32, (some, each), 0)
    c = lax.broadcasted_iota(jnp.int32, (some, each), 1)
    places = [
        jnp.where(
            c == r // part * blk + jnp.bitwise_xor(lax.axis_index("dp"), m) * part + r % part, 1.0, 0.0
        ).astype(BF16)
        for m in range(dp)
    ]
    wait_all(made[2])
    spans = [slice(m * rank_part, (m + 1) * rank_part) for m in range(dp)]
    for g in range(count // some):
        at = 2 * rows + g * some
        out = sum(nn(all_pieces[spans[m], at : at + some], places[m]) for m in range(dp))
        gdl[:, g * each : (g + 1) * each] = out.astype(BF16)
    wait_all(made[0])
    wait_all(made[1])
    lat_down = jnp.concatenate([all_pieces[m, :rows] for m in spans], axis=1)
    lat_pre = jnp.concatenate([all_pieces[m, rows : 2 * rows] for m in spans], axis=1)
    gdr[...] = (nn(lat_down, cot_all[...]) * scale).astype(BF16)
    gul[...] = (nn(lat_pre, tok_all[...]) * scale).astype(BF16)


def rank_pass(tok, cot, both, pieces, blk, scale):
    dp = len(pieces)
    rows, width = tok.shape
    rank_part, tall = pieces[0].shape
    args = [tok, cot, *both, *pieces]
    dims = [((dp * rows, width), BF16)] * 2 + [((dp * rank_part, tall), BF16)]
    wide = shape((rank_part, width))
    return pl.pallas_call(
        functools.partial(rank_kernel, dp, blk, scale),
        in_specs=[HBM] * len(args),
        out_specs=[VM] * 3,
        out_shape=[shape((rank_part, (tall - 2 * rows) * dp)), wide, wide],
        scratch_shapes=stacked(dims, 3 * dp),
        compiler_params=params(16),
        name="kr",
    )(*args)


def up_kernel(near, n_full, n_thin, first, dp, ratio, blk, rank_part, scale, *refs):
    take = iter(refs)
    pres = [next(take) for _ in range(2 * dp)]
    acts = [next(take) for _ in range(dp)]
    full = [[next(take)] for _ in range(1 + n_full)]
    gu, gur = next(take), next(take)
    groups = [acts] + full
    scratch = [next(take) for _ in groups]
    pre_all, lhs_all, sem = (next(take) for _ in range(3))
    copies = Copies(sem)
    made = gather_copies(groups, scratch, copies)
    part = gu.shape[2]
    rows, width = pres[0].shape
    late = [
        copies.start(ref, pre_all.at[pl.ds(m % dp * rows, rows), pl.ds(m // dp * width, width)])
        for m, ref in enumerate(pres)
    ]
    act_all, full_all = scratch[0], scratch[1:]
    blocks = full_all[0].shape[0] // part
    count = len(near) + n_full + n_thin
    step = count * part + rank_part
    for some in made:
        wait_all(some)
    for a in range(blocks):
        pieces = [full_all[0][(a ^ s) * part : ((a ^ s) + 1) * part, :] for s in near]
        pieces += [f[a * part : (a + 1) * part, :] for f in full_all[1:]]
        for j in range(n_thin):
            at = first + (j * blocks + a) * part
            pieces.append(act_all[at : at + part, :])
        pieces.append(act_all[act_all.shape[0] - rank_part :, :])
        lhs_all[a * step : (a + 1) * step, :] = jnp.concatenate(pieces, axis=0)
    wait_all(late)
    for a in range(blocks):
        for r in range(ratio):
            h = a * ratio + r
            out = nn(lhs_all[a * step : (a + 1) * step, :], pre_all[:, h * blk : (h + 1) * blk])
            out = (out * scale).astype(BF16)
            for j in range(count):
                gu[h, j] = out[j * part : (j + 1) * part]
            gur[:, h * blk : (h + 1) * blk] = out[count * part :]


def up_pass(pres, acts, n_thin, full, near, part, rank_part, scale, blk):
    dp = len(pres) // 2
    rows, hid = pres[0].shape[0], 2 * pres[0].shape[1]
    count = len(near) + len(full) - 1 + n_thin
    args = [*pres, *acts, *full]
    blocks = full[0].shape[0] // part
    dims = [((acts[0].shape[0], dp * rows), BF16)] + [(f.shape, BF16) for f in full]
    dims += [((dp * rows, hid), BF16), ((blocks * (count * part + rank_part), dp * rows), BF16)]
    first = hid // blk * part
    return pl.pallas_call(
        functools.partial(
            up_kernel, near, len(full) - 1, n_thin, first, dp, hid // (blocks * blk), blk, rank_part, scale
        ),
        in_specs=[HBM] * len(args),
        out_specs=[VM, VM],
        out_shape=[shape((hid // blk, count, part, blk)), shape((rank_part, hid))],
        scratch_shapes=stacked(dims, len(args)),
        compiler_params=params(20),
        name="ku",
    )(*args)


def shards(tokens, cotangent, up_blocks, down_blocks, up_left, up_right, down_left, down_right):
    rows, width = tokens.shape
    blk = up_blocks.shape[-1]
    blocks = width // blk
    dp = lax.axis_size("dp")
    part, rank_part = blk // dp, up_left.shape[1] // dp
    scale = 1.0 / math.sqrt(rows * dp)
    near = tuple(s for s in STRIDES if s < blocks)
    masks = [s // blocks for s in STRIDES if s >= blocks]
    bits = [1 << b for b in range(dp.bit_length() - 1)]
    flip = bits[::-1]
    thin = [i for i, m in enumerate(masks) if m != 1]
    tokens, cotangent, up_blocks, down_blocks = (in_hbm(x) for x in (tokens, cotangent, up_blocks, down_blocks))
    up_left, up_right, down_left, down_right = (in_hbm(x) for x in (up_left, up_right, down_left, down_right))

    tok_far = [swapped(tokens, "tensor", m) for m in masks]
    cot_far = [swapped(cotangent, "tensor", m) for m in masks]
    *lat_parts, both = latent_pass(tokens, cotangent, up_left, down_right)
    both = spread(both, bits)[1:]
    lat = total(*lat_parts)
    others, alone = join_pass(both)
    far = []
    for x, m in zip(cot_far, masks):
        if m == 1:
            far.append((x, swapped(others, "tensor", m), swapped(alone, "tensor", m)))
        elif m == 2:
            far.append((x, swapped(others, "tensor", m), swapped(x, "dp", dp // 2)))
        else:
            far.append(spread(x, flip))

    weights = (up_blocks, down_blocks, up_right, down_left)
    made = layer_half(dp, tuple(thin), tokens, tok_far, lat, *weights, near)
    acts, slope, out_here, out_parts, lat_down = made[:dp], made[dp], made[dp + 1], made[dp + 2 : -1], made[-1]
    made = layer_half(dp, (), cotangent, cot_far, lat, *weights, near, slope, lat_down)
    *pres, grad_here = made[:3]
    *grad_parts, lat_mine, lat_other = made[3:]
    out_parts = [swapped(x, "tensor", m) for x, m in zip(out_parts, masks)]
    grad_parts = [swapped(x, "tensor", m) for x, m in zip(grad_parts, masks)]
    act_groups = [x.reshape(-1, rows) for x in exchange(acts)]
    pre_groups = spread(pres[0], bits) + spread(pres[1], flip)
    hidden = up_blocks.shape[0]
    hidden = up_blocks.shape[0]
    *pieces, lat2, own_rows = cut_pass(
        total(lat_mine, lat_other), tokens, both, act_groups, hidden * part, part, rank_part, scale
    )
    pieces = exchange(pieces)
    gd = down_pass(cotangent, both, far, act_groups, hidden, near, part, scale, blk)
    gdl, gul, gdr = rank_pass(tokens, cotangent, both, pieces, blk, scale)
    layer_out, token_grads = finish_pass(lat2, down_right, up_left, out_here, grad_here, out_parts, grad_parts)
    full_rows = [own_rows] + [swapped(own_rows, "tensor", m) for m in masks if m == 1]
    gu, gur = up_pass(pre_groups, act_groups, len(thin), full_rows, near, part, rank_part, scale, blk)
    return layer_out, token_grads, gu, gd, gul.T, gur, gdl.T, gdr


def solution(mesh):
    d, t = "dp", "tensor"
    blocks = P(t, None, None, None)
    in_specs = (P(d, t), P(d, t), blocks, blocks, P(t, None), P(None, t), P(t, None), P(None, t))
    cut = P(t, None, d, None)
    out_specs = (P(d, t), P(d, t), cut, cut, P(t, d), P(d, t), P(t, d), P(d, t))
    return jax.shard_map(shards, mesh=mesh, in_specs=in_specs, out_specs=out_specs, check_vma=False)
```
